32 devices in a mesh: groups: 2 (over y), ctx: 16 (over z, x, core), head: 1.
Axes of the slice: x: 2, y: 2, z: 4, core: 2. Of those that a mesh axis runs over, the one named last changes fastest.
Arguments:
- queries: bfloat16 [4096, 4096], P(('groups', 'ctx'), 'head'), parts along dimension 0, may hold values from -8 to 8
- keys: bfloat16 [4096, 1024], P(('groups', 'ctx'), 'head'), parts along dimension 0, may hold values from -8 to 8
- values: bfloat16 [4096, 1024], P(('groups', 'ctx'), 'head'), parts along dimension 0, may hold values from -6 to 6
- grad_out: bfloat16 [4096, 4096], P(('groups', 'ctx'), 'head'), parts along dimension 0, may hold values from -6 to 6
Outputs:
- grad_queries: bfloat16 [4096, 4096], P(('groups', 'ctx'), 'head'), parts along dimension 0
- grad_keys: bfloat16 [4096, 1024], P(('groups', 'ctx'), 'head'), parts along dimension 0
- grad_values: bfloat16 [4096, 1024], P(('groups', 'ctx'), 'head'), parts along dimension 0
- log_norm: float32 [4096, 32], P(('groups', 'ctx'), 'head'), parts along dimension 0
The draws below stay inside these ranges and needn't reach their ends.
There are 2 independent parts, one for each index of `groups`. The reference program is written for one: setup_inputs(seed, part) draws one part's arguments, and reference() takes and returns one part's arrays. A program takes and returns all parts, laid end to end along the dimension named above; each array names one. Nothing has to cross between parts.
All inputs are finite; a program needn't handle non-finite values.
Results may differ from the reference program's by a relative error of at most 0.0099.
Values may be sent and summed in bfloat16 or wider, within the bound.
No kernel may reach another device: no remote copies, remote signals or barrier semaphores. Data moves between devices by JAX's collectives and lax.ppermute only.
A program may use at most 64 MiB of HBM per device.

```python
import math
import jax
import jax.numpy as jnp
from jax import lax

QUERY_HEADS = 32
KEY_VALUE_HEADS = 8
HEAD_SIZE = 128
W = 512
STRIDE = 128
S_DEV = 128
TOKEN_COUNT = 2048
NSTRIDE = 16
N_CTX = 16


def draw_queries(key, part):
    noise_seed = jax.random.fold_in(jax.random.fold_in(key, 11), 0)
    drawn_values = jnp.clip(1.5 * jax.random.normal(noise_seed, (TOKEN_COUNT, QUERY_HEADS * HEAD_SIZE), jnp.float32), -8.0, 8.0)
    return drawn_values.astype(jnp.bfloat16)


def draw_keys(key, part):
    noise_seed = jax.random.fold_in(jax.random.fold_in(key, 23), 0)
    drawn_values = jnp.clip(jax.random.normal(noise_seed, (TOKEN_COUNT, KEY_VALUE_HEADS * HEAD_SIZE), jnp.float32), -6.0, 6.0)
    return drawn_values.astype(jnp.bfloat16)


def level_of(rng, extent, cuts, least, largest):
    loudness, own = 1.0, jax.random.fold_in(rng, 6)
    for axis_at, parts in cuts:
        steps = jnp.exp(jax.random.uniform(jax.random.fold_in(own, axis_at), (parts,), jnp.float32, least / len(cuts), largest / len(cuts)))
        loudness = loudness * jnp.repeat(steps, extent[axis_at] // parts).reshape([-1 if axis == axis_at else 1 for axis in range(len(extent))])
    return loudness


def gaussian(key, dims, scale, limit, cuts=(), held_as=jnp.bfloat16):
    entries = jax.random.normal(key, dims, jnp.float32) * scale
    if len(cuts) > 0:
        entries = level_of(key, dims, cuts, -0.22, 0.18) * entries
    return jnp.clip(entries, min=-limit, max=limit).astype(held_as)


def setup_inputs(seed: int = 0, part: int = 0) -> dict:
    arg_keys = jax.random.split(jax.random.key(seed), 5)
    part_splits = jax.random.split(jax.random.fold_in(arg_keys[4], part), 5)
    queries = draw_queries(jax.random.fold_in(jax.random.fold_in(arg_keys[4], part), 71), part)
    keys = draw_keys(jax.random.fold_in(jax.random.fold_in(arg_keys[4], part), 71), part)
    values = gaussian(part_splits[2], (TOKEN_COUNT, KEY_VALUE_HEADS * HEAD_SIZE), 1.0, 6.0, ((0, 16),))
    grad_out = gaussian(part_splits[3], (TOKEN_COUNT, QUERY_HEADS * HEAD_SIZE), 1.0, 6.0, ((0, 16),))
    return dict(queries=queries, keys=keys, values=values, grad_out=grad_out)


NEG_FILL = -1e+30

def attend_block(query_matrix, gradient_rows, key_matrix, value_matrix, allowed):
    token_rows = query_matrix.shape[0]
    heads_per_group = QUERY_HEADS // KEY_VALUE_HEADS
    scale_factor = 1.0 / math.sqrt(HEAD_SIZE)
    query_float = query_matrix.reshape(token_rows, KEY_VALUE_HEADS, heads_per_group, HEAD_SIZE).astype(jnp.float32)
    gradient_fn = gradient_rows.reshape(token_rows, KEY_VALUE_HEADS, heads_per_group, HEAD_SIZE).astype(jnp.float32)
    key_float = key_matrix.reshape(-1, KEY_VALUE_HEADS, HEAD_SIZE).astype(jnp.float32)
    value_float = value_matrix.reshape(-1, KEY_VALUE_HEADS, HEAD_SIZE).astype(jnp.float32)
    scores = jnp.einsum('qgrd,kgd->grqk', query_float, key_float) * scale_factor
    scores = jnp.where(allowed, scores, NEG_FILL)
    top_score = lax.optimization_barrier(jnp.max(scores, axis=-1))
    log_norm = top_score + jnp.log(lax.optimization_barrier(jnp.sum(jnp.exp(scores - top_score[..., None]), axis=-1)))
    probs = jnp.exp(scores - log_norm[..., None])
    probability_lowp = probs.astype(jnp.bfloat16)
    attended = jnp.einsum('grqk,kgd->qgrd', probability_lowp.astype(jnp.float32), value_float)
    delta_rows = lax.optimization_barrier(jnp.sum(gradient_fn * attended, axis=-1))
    dprobs = jnp.einsum('qgrd,kgd->grqk', gradient_fn, value_float)
    score_gradient = (probs * (dprobs - jnp.transpose(delta_rows, (1, 2, 0))[..., None]) * scale_factor).astype(jnp.bfloat16)
    grad_query = jnp.einsum('grqk,kgd->qgrd', score_gradient.astype(jnp.float32), key_float)
    grad_query = grad_query.astype(jnp.bfloat16).reshape(token_rows, QUERY_HEADS * HEAD_SIZE)
    key_gradient = jnp.einsum('yvtf,tyvp->fyp', score_gradient.astype(jnp.float32), query_float).reshape(-1, KEY_VALUE_HEADS * HEAD_SIZE)
    value_gradient = jnp.einsum('yvtf,tyvp->fyp', probability_lowp.astype(jnp.float32), gradient_fn).reshape(-1, KEY_VALUE_HEADS * HEAD_SIZE)
    norm_rows = jnp.transpose(log_norm, (2, 0, 1)).reshape(token_rows, QUERY_HEADS)
    return (grad_query, norm_rows, key_gradient, value_gradient)

def add_strided(total, extra):
    shaped = total.reshape(NSTRIDE, STRIDE, -1)
    head_rows = shaped[:, :1] + extra[:, None]
    return jnp.concatenate([head_rows, shaped[:, 1:]], axis=1).reshape(TOKEN_COUNT, -1)

def reference(queries, keys, values, grad_out):
    hops = (W + S_DEV - 1) // S_DEV
    win_len = (hops + 1) * S_DEV
    lead = hops * S_DEV
    key_value_width = KEY_VALUE_HEADS * HEAD_SIZE
    key_pad = jnp.concatenate([jnp.zeros((lead, key_value_width), keys.dtype), keys], axis=0)
    value_pad = jnp.concatenate([jnp.zeros((lead, key_value_width), values.dtype), values], axis=0)
    strided_keys = keys.reshape(NSTRIDE, STRIDE, key_value_width)[:, 0]
    strided_values = values.reshape(NSTRIDE, STRIDE, key_value_width)[:, 0]
    strided_pos = jnp.arange(NSTRIDE).astype(jnp.int32) * STRIDE
    offsets = jnp.arange(S_DEV).astype(jnp.int32)
    win_offsets = jnp.arange(win_len).astype(jnp.int32)

    def one_block(carry, block):
        key_grads, value_grads, strided_kg, strided_vg = carry
        first = (block * S_DEV).astype(jnp.int32)
        query_matrix = lax.dynamic_slice_in_dim(queries, first, S_DEV, 0)
        gradient_rows = lax.dynamic_slice_in_dim(grad_out, first, S_DEV, 0)
        win_keys = lax.dynamic_slice_in_dim(key_pad, first, win_len, 0)
        win_values = lax.dynamic_slice_in_dim(value_pad, first, win_len, 0)
        later = (first + offsets)[:, None]
        key_pos = (first - lead + win_offsets)[None, :]
        in_window = (key_pos >= 0) & (key_pos <= later) & (later - key_pos < W) & (key_pos % STRIDE != 0)
        in_stride = strided_pos[None, :] <= later
        allowed = jnp.concatenate([in_window, in_stride], axis=1)
        grad_query, norm_rows, key_gradient, value_gradient = attend_block(query_matrix, gradient_rows, jnp.concatenate([win_keys, strided_keys], axis=0), jnp.concatenate([win_values, strided_values], axis=0), allowed)
        current_k = lax.dynamic_slice_in_dim(key_grads, first, win_len, 0)
        key_grads = lax.dynamic_update_slice_in_dim(key_grads, current_k + key_gradient[:win_len], first, 0)
        current_v = lax.dynamic_slice_in_dim(value_grads, first, win_len, 0)
        value_grads = lax.dynamic_update_slice_in_dim(value_grads, current_v + value_gradient[:win_len], first, 0)
        strided_kg = strided_kg + key_gradient[win_len:]
        strided_vg = strided_vg + value_gradient[win_len:]
        return ((key_grads, value_grads, strided_kg, strided_vg), (grad_query, norm_rows))
    start_state = (jnp.zeros((lead + TOKEN_COUNT, key_value_width), jnp.float32), jnp.zeros((lead + TOKEN_COUNT, key_value_width), jnp.float32), jnp.zeros((NSTRIDE, key_value_width), jnp.float32), jnp.zeros((NSTRIDE, key_value_width), jnp.float32))
    final_state, stacked = lax.scan(one_block, start_state, jnp.arange(N_CTX).astype(jnp.int32))
    key_grads, value_grads, strided_kg, strided_vg = final_state
    grad_keys = add_strided(key_grads[lead:], strided_kg).astype(jnp.bfloat16)
    grad_values = add_strided(value_grads[lead:], strided_vg).astype(jnp.bfloat16)
    grad_queries = stacked[0].reshape(TOKEN_COUNT, QUERY_HEADS * HEAD_SIZE)
    log_norm = stacked[1].reshape(TOKEN_COUNT, QUERY_HEADS)
    return (grad_queries, grad_keys, grad_values, log_norm)
```

```python
import functools
import math

import jax
import jax.numpy as jnp
from jax import lax
from jax.experimental import pallas as pl
from jax.experimental.pallas import tpu as pltpu
from jax.sharding import PartitionSpec as P

HEAD_SIZE = 128
W = 512
STRIDE = 128
CHUNKS = 2

NEG_FILL = -1e30
SCALE = 1.0 / math.sqrt(HEAD_SIZE)


def dot_nt(left, right):
    return lax.dot_general(
        left, right, (((1,), (1,)), ((), ())), preferred_element_type=jnp.float32
    )


def dot_nn(left, right):
    return lax.dot_general(
        left, right, (((1,), (0,)), ((), ())), preferred_element_type=jnp.float32
    )


def dot_tn(left, right):
    return lax.dot_general(
        left, right, (((0,), (0,)), ((), ())), preferred_element_type=jnp.float32
    )


def attention_kernel(
    place,
    q_own,
    q_other,
    o_own,
    o_other,
    kv_here,
    kv_near,
    kv_past,
    kv_far,
    dq_own,
    dq_other,
    norm,
    g_here,
    g_near,
    g_past,
    g_far,
):
    half = q_own.shape[0]
    rows = 2 * half
    far_rows = kv_far.shape[0]
    heads = q_own.shape[1] // HEAD_SIZE
    core, pair = place[0], place[1]

    def token(shape, axis):
        at = lax.broadcasted_iota(jnp.int32, shape, axis)
        return at + jnp.where(at < half, core * half, -core * half)

    lower = token((rows, rows), 0) <= token((rows, rows), 1)
    far_at = lax.broadcasted_iota(jnp.int32, (far_rows, rows), 0)
    far_token = (far_at // 2) * rows + jnp.where(far_at % 2 == 0, core, 1 - core) * half
    far_open = far_token <= pair * rows + token((far_rows, rows), 1) - W
    near_bias = jnp.where(pair >= 1, 0.0, NEG_FILL)
    past_bias = jnp.where(pair >= 2, 0.0, NEG_FILL)

    def stacked(side):
        columns = slice(side * HEAD_SIZE, (side + 1) * HEAD_SIZE)
        return jnp.concatenate(
            [kv_here[:, columns], kv_near[:, columns], kv_past[:, columns], kv_far[:, columns]],
            axis=0,
        )

    key_all, value_all = stacked(0), stacked(1)
    key_terms = value_terms = None

    for head in range(heads):
        columns = slice(head * HEAD_SIZE, (head + 1) * HEAD_SIZE)
        query = jnp.concatenate([q_own[:, columns], q_other[:, columns]], axis=0)
        grad = jnp.concatenate([o_own[:, columns], o_other[:, columns]], axis=0)
        score = dot_nt(key_all, query)
        edge = jnp.where(lower, score[:rows], score[2 * rows : 3 * rows] + past_bias)
        near = score[rows : 2 * rows] + near_bias
        far = jnp.where(far_open, score[3 * rows :], NEG_FILL)
        top = jnp.maximum(
            jnp.maximum(
                jnp.max(edge, axis=0, keepdims=True), jnp.max(near, axis=0, keepdims=True)
            ),
            jnp.max(far, axis=0, keepdims=True),
        )
        edge, near, far = (
            jnp.exp2((part - top) * (SCALE * math.log2(math.e))) for part in (edge, near, far)
        )
        total = (
            jnp.sum(edge, axis=0, keepdims=True)
            + jnp.sum(near, axis=0, keepdims=True)
            + jnp.sum(far, axis=0, keepdims=True)
        )
        norm[head : head + 1, :] = top * SCALE + jnp.log(total)
        inverse = 1.0 / total
        edge, near, far = (part * inverse for part in (edge, near, far))
        dprob = dot_nt(value_all, grad)
        d_edge = jnp.where(lower, dprob[:rows], dprob[2 * rows : 3 * rows])
        d_near = dprob[rows : 2 * rows]
        d_far = dprob[3 * rows :]
        delta = (
            jnp.sum(edge * d_edge, axis=0, keepdims=True)
            + jnp.sum(near * d_near, axis=0, keepdims=True)
            + jnp.sum(far * d_far, axis=0, keepdims=True)
        )
        d_edge, d_near, d_far = (
            part * (d_part - delta)
            for part, d_part in ((edge, d_edge), (near, d_near), (far, d_far))
        )

        def split(on_edge, on_near, on_far):
            return jnp.concatenate(
                [
                    jnp.where(lower, on_edge, 0.0).astype(jnp.bfloat16),
                    on_near.astype(jnp.bfloat16),
                    jnp.where(lower, 0.0, on_edge).astype(jnp.bfloat16),
                    on_far.astype(jnp.bfloat16),
                ],
                axis=0,
            )

        prob = split(edge, near, far)
        dscore = split(d_edge, d_near, d_far)
        value_term = dot_nn(prob, grad)
        key_term = dot_nn(dscore, query)
        value_terms = value_term if head == 0 else value_terms + value_term
        key_terms = key_term if head == 0 else key_terms + key_term
        query_term = (dot_tn(dscore, key_all) * SCALE).astype(jnp.bfloat16)
        dq_own[:, columns] = query_term[:half]
        dq_other[:, columns] = query_term[half:]

    terms = jnp.concatenate([key_terms * SCALE, value_terms], axis=1)
    g_here[...] = terms[:rows]
    g_near[...] = terms[rows : 2 * rows].astype(jnp.bfloat16)
    g_past[...] = terms[2 * rows : 3 * rows].astype(jnp.bfloat16)
    g_far[...] = terms[3 * rows :]


def attention(place, queries, q_other, grad_out, o_other, kv_here, kv_near, kv_past, kv_far, chunk):
    half = queries.shape[0]
    rows = 2 * half
    far_rows = kv_far.shape[0]
    both = 2 * HEAD_SIZE
    count = kv_here.shape[1] // both
    group_width = q_other.shape[1] // (count * CHUNKS)
    heads = group_width // HEAD_SIZE
    first = chunk * count
    per_core = count * CHUNKS

    own = pl.BlockSpec((half, group_width), lambda h, place: (0, place[0] * per_core + first + h))
    other = pl.BlockSpec((half, group_width), lambda h, place: (0, first + h))
    block = pl.BlockSpec((rows, both), lambda h, place: (0, h))
    out = pl.BlockSpec((half, group_width), lambda h, place: (0, h))
    far_in = pl.BlockSpec((far_rows, both), lambda h, place: (0, first + h))
    far_out = pl.BlockSpec((far_rows, both), lambda h, place: (0, h))
    keys_seen = 3 * rows + far_rows
    return pl.pallas_call(
        attention_kernel,
        name=f"attention_{chunk}",
        grid_spec=pltpu.PrefetchScalarGridSpec(
            num_scalar_prefetch=1,
            grid=(count,),
            in_specs=[own, other, own, other, block, block, block, far_in],
            out_specs=[
                out,
                out,
                pl.BlockSpec((None, heads, rows), lambda h, place: (h, 0, 0)),
                block,
                block,
                block,
                far_out,
            ],
        ),
        out_shape=[
            jax.ShapeDtypeStruct((half, count * group_width), jnp.bfloat16),
            jax.ShapeDtypeStruct((half, count * group_width), jnp.bfloat16),
            jax.ShapeDtypeStruct((count, heads, rows), jnp.float32),
            jax.ShapeDtypeStruct((rows, count * both), jnp.float32),
            jax.ShapeDtypeStruct((rows, count * both), jnp.bfloat16),
            jax.ShapeDtypeStruct((rows, count * both), jnp.bfloat16),
            jax.ShapeDtypeStruct((far_rows, count * both), jnp.float32),
        ],
        compiler_params=pltpu.CompilerParams(vmem_limit_bytes=40 * 1024 * 1024),
        cost_estimate=pl.CostEstimate(
            flops=count * heads * rows * keys_seen * HEAD_SIZE * 10,
            transcendentals=count * heads * rows * keys_seen,
            bytes_accessed=count * (6 * half * group_width * 2 + 5 * rows * both * 4),
        ),
    )(place, queries, q_other, grad_out, o_other, kv_here, kv_near, kv_past, kv_far)


def local(queries, keys, values, grad_out):
    half, kv_width = keys.shape
    kv_heads = kv_width // HEAD_SIZE
    both = 2 * HEAD_SIZE
    group_width = queries.shape[1] // kv_heads
    rows = 2 * half
    peers = lax.axis_size("ctx")
    pairs = peers // 2
    assert half == STRIDE and W == 2 * rows and peers % 2 == 0 and kv_heads % (2 * CHUNKS) == 0
    per_core = kv_heads // 2
    count = per_core // CHUNKS
    index = lax.axis_index("ctx")
    core, pair = index % 2, index // 2
    place = jnp.stack([core, pair]).astype(jnp.int32)

    def swap(x):
        return lax.ppermute(x, "ctx", [(i, i ^ 1) for i in range(peers)])

    def shifted(x, by):
        return lax.ppermute(x, "ctx", [(i, i + by) for i in range(peers) if 0 <= i + by < peers])

    def exchanged(x):
        groups = [list(range(parity, peers, 2)) for parity in range(2)]
        return lax.all_to_all(x, "ctx", 0, 0, axis_index_groups=groups, tiled=True)

    def part(x, which, width):
        return lax.dynamic_slice_in_dim(x, which * width, width, 1)

    def joined(mine, theirs):
        return jnp.where(
            core == 0,
            jnp.concatenate([mine, theirs], axis=1),
            jnp.concatenate([theirs, mine], axis=1),
        )

    key_value = jnp.stack(
        [keys.reshape(half, kv_heads, HEAD_SIZE), values.reshape(half, kv_heads, HEAD_SIZE)], axis=2
    ).reshape(half, kv_heads * both)
    kv_mine = part(key_value, core, per_core * both)
    kv_other = swap(part(key_value, 1 - core, per_core * both))

    here, near, past = [], [], []
    for chunk in range(CHUNKS):
        columns = slice(chunk * count * both, (chunk + 1) * count * both)
        here.append(jnp.concatenate([kv_mine[:, columns], kv_other[:, columns]], axis=0))
        near.append(shifted(here[chunk], 2))
        past.append(shifted(here[chunk], 4))
    strided = jnp.concatenate([kv_mine[:1], kv_other[:1]], axis=1)
    far = exchanged(jnp.broadcast_to(strided, (pairs, 2 * per_core * both)))
    far = far.reshape(2 * pairs, per_core * both)
    q_other = swap(part(queries, 1 - core, per_core * group_width))
    o_other = swap(part(grad_out, 1 - core, per_core * group_width))

    dq_own, dq_other, norms, sums, far_terms = [], [], [], [], []
    for chunk in range(CHUNKS):
        out = attention(
            place,
            queries,
            q_other,
            grad_out,
            o_other,
            here[chunk],
            near[chunk],
            past[chunk],
            far,
            chunk,
        )
        dq_own.append(out[0])
        dq_other.append(swap(out[1]))
        norms.append(out[2])
        near_terms, past_terms = shifted(out[4], -2), shifted(out[5], -4)
        sums.append((out[3], near_terms, past_terms))
        far_terms.append(out[6])

    far_terms = jnp.concatenate(far_terms, axis=1).reshape(pairs, 2 * per_core * both)
    strided_sum = jnp.sum(exchanged(far_terms), axis=0).reshape(2, per_core * both)
    row = lax.broadcasted_iota(jnp.int32, (rows, 1), 0)
    total = jnp.concatenate(
        [a + b.astype(jnp.float32) + c.astype(jnp.float32) for a, b, c in sums], axis=1
    )
    total = (
        total
        + jnp.where(row == 0, strided_sum[:1], 0.0)
        + jnp.where(row == half, strided_sum[1:], 0.0)
    ).astype(jnp.bfloat16)
    grads = joined(total[:half], swap(total[half:])).reshape(half, kv_heads, 2, HEAD_SIZE)
    grad_keys = grads[:, :, 0].reshape(half, kv_width)
    grad_values = grads[:, :, 1].reshape(half, kv_width)
    grad_queries = joined(jnp.concatenate(dq_own, axis=1), jnp.concatenate(dq_other, axis=1))
    norm = jnp.concatenate(norms, axis=0).reshape(-1, rows)
    log_norm = joined(norm[:, :half].T, swap(norm[:, half:]).T)
    return (grad_queries, grad_keys, grad_values, log_norm)


def solution(mesh):
    placed = P(("groups", "ctx"), "head")
    return jax.shard_map(
        local,
        mesh=mesh,
        in_specs=(placed,) * 4,
        out_specs=(placed,) * 4,
        check_vma=False,
    )
```

```python
import functools
import math

import jax
import jax.numpy as jnp
from jax import lax
from jax.experimental import pallas as pl
from jax.experimental.pallas import tpu as pltpu
from jax.sharding import PartitionSpec as P

HEAD_SIZE = 128
W = 512
STRIDE = 128
CHUNKS = 2

NEG_FILL = -1e30
SCALE = 1.0 / math.sqrt(HEAD_SIZE)


def vmem_shape(shape, dtype):
    return pltpu.VMEM(shape, dtype)


def in_vmem(*arrays):
    return [pltpu.with_memory_space_constraint(x, pltpu.VMEM) for x in arrays]


def head_columns(which, width=HEAD_SIZE):
    return pl.ds(pl.multiple_of(which * width, width), width)


def dot_nt(left, right):
    return lax.dot_general(
        left, right, (((1,), (1,)), ((), ())), preferred_element_type=jnp.float32
    )


def dot_nn(left, right):
    return lax.dot_general(
        left, right, (((1,), (0,)), ((), ())), preferred_element_type=jnp.float32
    )


def dot_tn(left, right):
    return lax.dot_general(
        left, right, (((0,), (0,)), ((), ())), preferred_element_type=jnp.float32
    )


def attention_kernel(
    chunk,
    place,
    q_own,
    q_other,
    o_own,
    o_other,
    kv_here,
    kv_near,
    kv_past,
    kv_far,
    dq_own,
    dq_other,
    norm,
    g_here,
    g_near,
    g_past,
    g_far,
):
    half = q_own.shape[0]
    rows = 2 * half
    far_rows = kv_far.shape[0]
    count = kv_here.shape[1] // (2 * HEAD_SIZE)
    heads = dq_own.shape[1] // (count * HEAD_SIZE)
    core, pair = place[0], place[1]

    def token(shape, axis):
        at = lax.broadcasted_iota(jnp.int32, shape, axis)
        return at + jnp.where(at < half, core * half, -core * half)

    lower = token((rows, rows), 0) <= token((rows, rows), 1)
    far_at = lax.broadcasted_iota(jnp.int32, (far_rows, rows), 0)
    far_token = (far_at // 2) * rows + jnp.where(far_at % 2 == 0, core, 1 - core) * half
    far_open = far_token <= pair * rows + token((far_rows, rows), 1) - W
    near_bias = jnp.where(pair >= 1, 0.0, NEG_FILL)
    past_bias = jnp.where(pair >= 2, 0.0, NEG_FILL)

    def stacked(at, side):
        columns = slice((2 * at + side) * HEAD_SIZE, (2 * at + side + 1) * HEAD_SIZE)
        start = (2 * (chunk * count + at) + side) * HEAD_SIZE
        return jnp.concatenate(
            [
                kv_here[:, columns],
                kv_near[:, columns],
                kv_past[:, columns],
                kv_far[:, start : start + HEAD_SIZE],
            ],
            axis=0,
        )

    for at in range(count):
        key_all, value_all = stacked(at, 0), stacked(at, 1)
        key_terms = value_terms = None

        for head in range(heads):
            columns = slice((at * heads + head) * HEAD_SIZE, (at * heads + head + 1) * HEAD_SIZE)
            source = head_columns((core * (count * CHUNKS) + chunk * count + at) * heads + head)
            query = jnp.concatenate([q_own[:, source], q_other[:, source]], axis=0)
            grad = jnp.concatenate([o_own[:, source], o_other[:, source]], axis=0)
            score = dot_nt(key_all, query)
            edge = jnp.where(lower, score[:rows], score[2 * rows : 3 * rows] + past_bias)
            near = score[rows : 2 * rows] + near_bias
            far = jnp.where(far_open, score[3 * rows :], NEG_FILL)
            top = jnp.maximum(
                jnp.maximum(
                    jnp.max(edge, axis=0, keepdims=True), jnp.max(near, axis=0, keepdims=True)
                ),
                jnp.max(far, axis=0, keepdims=True),
            )
            edge, near, far = (
                jnp.exp2((part - top) * (SCALE * math.log2(math.e))) for part in (edge, near, far)
            )
            total = (
                jnp.sum(edge, axis=0, keepdims=True)
                + jnp.sum(near, axis=0, keepdims=True)
                + jnp.sum(far, axis=0, keepdims=True)
            )
            norm[at * heads + head : at * heads + head + 1, :] = top * SCALE + jnp.log(total)
            inverse = 1.0 / total
            edge, near, far = (part * inverse for part in (edge, near, far))
            dprob = dot_nt(value_all, grad)
            d_edge = jnp.where(lower, dprob[:rows], dprob[2 * rows : 3 * rows])
            d_near = dprob[rows : 2 * rows]
            d_far = dprob[3 * rows :]
            delta = (
                jnp.sum(edge * d_edge, axis=0, keepdims=True)
                + jnp.sum(near * d_near, axis=0, keepdims=True)
                + jnp.sum(far * d_far, axis=0, keepdims=True)
            )
            d_edge, d_near, d_far = (
                part * (d_part - delta)
                for part, d_part in ((edge, d_edge), (near, d_near), (far, d_far))
            )

            def split(on_edge, on_near, on_far):
                return jnp.concatenate(
                    [
                        jnp.where(lower, on_edge, 0.0).astype(jnp.bfloat16),
                        on_near.astype(jnp.bfloat16),
                        jnp.where(lower, 0.0, on_edge).astype(jnp.bfloat16),
                        on_far.astype(jnp.bfloat16),
                    ],
                    axis=0,
                )

            prob = split(edge, near, far)
            dscore = split(d_edge, d_near, d_far)
            value_term = dot_nn(prob, grad)
            key_term = dot_nn(dscore, query)
            value_terms = value_term if head == 0 else value_terms + value_term
            key_terms = key_term if head == 0 else key_terms + key_term
            query_term = (dot_tn(dscore, key_all) * SCALE).astype(jnp.bfloat16)
            dq_own[:, columns] = query_term[:half]
            dq_other[:, columns] = query_term[half:]

        terms = jnp.concatenate([key_terms * SCALE, value_terms], axis=1)
        columns = slice(2 * at * HEAD_SIZE, 2 * (at + 1) * HEAD_SIZE)
        g_here[:, columns] = terms[:rows]
        g_near[:, columns] = terms[rows : 2 * rows].astype(jnp.bfloat16)
        g_past[:, columns] = terms[2 * rows : 3 * rows].astype(jnp.bfloat16)
        g_far[:, columns] = terms[3 * rows :]


def attention(place, queries, q_other, grad_out, o_other, kv_here, kv_near, kv_past, kv_far, chunk):
    half = queries.shape[0]
    rows = 2 * half
    far_rows = kv_far.shape[0]
    both = 2 * HEAD_SIZE
    count = kv_here.shape[1] // both
    per_core = count * CHUNKS
    group_width = queries.shape[1] // (2 * per_core)
    heads = group_width // HEAD_SIZE

    whole = pl.BlockSpec(memory_space=pltpu.VMEM)
    keys_seen = 3 * rows + far_rows
    return pl.pallas_call(
        functools.partial(attention_kernel, chunk),
        name=f"attention_{chunk}",
        in_specs=[pl.BlockSpec(memory_space=pltpu.SMEM)] + [whole] * 8,
        out_specs=[whole] * 7,
        out_shape=[
            vmem_shape((half, count * group_width), jnp.bfloat16),
            vmem_shape((half, count * group_width), jnp.bfloat16),
            vmem_shape((count * heads, rows), jnp.float32),
            vmem_shape((rows, count * both), jnp.float32),
            vmem_shape((rows, count * both), jnp.bfloat16),
            vmem_shape((rows, count * both), jnp.bfloat16),
            vmem_shape((far_rows, count * both), jnp.float32),
        ],
        compiler_params=pltpu.CompilerParams(vmem_limit_bytes=20 * 1024 * 1024),
        cost_estimate=pl.CostEstimate(
            flops=count * heads * rows * keys_seen * HEAD_SIZE * 20,
            transcendentals=count * heads * rows * keys_seen,
            bytes_accessed=count * (6 * half * group_width * 2 + 5 * rows * both * 4),
        ),
    )(place, *in_vmem(queries, q_other, grad_out, o_other, kv_here, kv_near, kv_past, kv_far))


def arrange_kernel(place, keys, values, k_other, v_other, *outs):
    half = keys.shape[0]
    *payloads, strided = outs
    count = payloads[0].shape[1] // (2 * HEAD_SIZE)
    for chunk, payload in enumerate(payloads):
        for h in range(count):
            source = head_columns(place[0] * (count * CHUNKS) + chunk * count + h)
            for side, (mine, theirs) in enumerate(((keys, k_other), (values, v_other))):
                to = slice((2 * h + side) * HEAD_SIZE, (2 * h + side + 1) * HEAD_SIZE)
                payload[:half, to] = mine[:, source]
                payload[half:, to] = theirs[:, source]
        width = payload.shape[1]
        strided[0:1, chunk * width : (chunk + 1) * width] = payload[0:1, :]
        strided[1:2, chunk * width : (chunk + 1) * width] = payload[half : half + 1, :]


def arrange(place, keys, values, k_other, v_other):
    half, kv_width = keys.shape
    whole = pl.BlockSpec(memory_space=pltpu.VMEM)
    payload = vmem_shape((2 * half, kv_width // CHUNKS), keys.dtype)
    return pl.pallas_call(
        arrange_kernel,
        name="arrange",
        in_specs=[pl.BlockSpec(memory_space=pltpu.SMEM)] + [whole] * 4,
        out_specs=[whole] * (CHUNKS + 1),
        out_shape=[payload] * CHUNKS + [vmem_shape((2, kv_width), keys.dtype)],
    )(place, *in_vmem(keys, values, k_other, v_other))


def collect_kernel(chunk, here, near, past, strided, mine, theirs):
    half, width = mine.shape
    extra = jnp.sum(strided[:, :, chunk * width : (chunk + 1) * width], axis=0)
    total = here[...] + near[...].astype(jnp.float32) + past[...].astype(jnp.float32)
    row = lax.broadcasted_iota(jnp.int32, (half, 1), 0)
    mine[...] = (total[:half] + jnp.where(row == 0, extra[0:1], 0.0)).astype(mine.dtype)
    theirs[...] = (total[half:] + jnp.where(row == 0, extra[1:2], 0.0)).astype(theirs.dtype)


def collect(here, near, past, strided, chunk):
    rows, width = here.shape
    half = vmem_shape((rows // 2, width), jnp.bfloat16)
    whole = pl.BlockSpec(memory_space=pltpu.VMEM)
    return pl.pallas_call(
        functools.partial(collect_kernel, chunk),
        name=f"collect_{chunk}",
        in_specs=[whole] * 4,
        out_specs=[whole, whole],
        out_shape=[half, half],
        cost_estimate=pl.CostEstimate(
            flops=rows * width * 4, transcendentals=0, bytes_accessed=rows * width * 10
        ),
    )(*in_vmem(here, near, past, strided))


def place_kernel(place, *refs):
    *parts, grad_keys, grad_values = refs
    count = parts[0].shape[1] // (2 * HEAD_SIZE)
    for chunk in range(CHUNKS):
        mine, theirs = parts[2 * chunk : 2 * chunk + 2]
        for h in range(count):
            at = chunk * count + h
            for core, block in ((place[0], mine), (1 - place[0], theirs)):
                to = head_columns(core * (count * CHUNKS) + at)
                grad_keys[:, to] = block[:, 2 * h * HEAD_SIZE : (2 * h + 1) * HEAD_SIZE]
                grad_values[:, to] = block[:, (2 * h + 1) * HEAD_SIZE : (2 * h + 2) * HEAD_SIZE]


def placed_grads(place, parts, half, kv_width):
    whole = pl.BlockSpec(memory_space=pltpu.VMEM)
    out = jax.ShapeDtypeStruct((half, kv_width), jnp.bfloat16)
    return pl.pallas_call(
        place_kernel,
        name="place",
        in_specs=[pl.BlockSpec(memory_space=pltpu.SMEM)] + [whole] * len(parts),
        out_specs=[whole, whole],
        out_shape=[out, out],
    )(place, *in_vmem(*parts))


def local(queries, keys, values, grad_out):
    half, kv_width = keys.shape
    kv_heads = kv_width // HEAD_SIZE
    rows = 2 * half
    peers = lax.axis_size("ctx")
    pairs = peers // 2
    assert half == STRIDE and W == 2 * rows and peers % 2 == 0 and kv_heads % (2 * CHUNKS) == 0
    index = lax.axis_index("ctx")
    core, pair = index & 1, index >> 1
    place = jnp.stack([core, pair]).astype(jnp.int32)

    def swap(x):
        return lax.ppermute(x, "ctx", [(i, i ^ 1) for i in range(peers)])

    def shifted(x, by):
        return lax.ppermute(x, "ctx", [(i, i + by) for i in range(peers) if 0 <= i + by < peers])

    def exchanged(x):
        groups = [list(range(parity, peers, 2)) for parity in range(2)]
        return lax.all_to_all(x, "ctx", 0, 0, axis_index_groups=groups)

    def joined(mine, theirs):
        return jnp.where(
            core == 0,
            jnp.concatenate([mine, theirs], axis=1),
            jnp.concatenate([theirs, mine], axis=1),
        )

    *here, strided = arrange(place, keys, values, swap(keys), swap(values))
    near = [shifted(payload, 2) for payload in here]
    past = [shifted(payload, 4) for payload in here]
    far = exchanged(jnp.broadcast_to(strided[None], (pairs, 2, kv_width)))
    far = far.reshape(2 * pairs, kv_width)
    q_other, o_other = swap(queries), swap(grad_out)

    dq_own, dq_other, norms, sums, far_terms = [], [], [], [], []
    for chunk in range(CHUNKS):
        out = attention(
            place,
            queries,
            q_other,
            grad_out,
            o_other,
            here[chunk],
            near[chunk],
            past[chunk],
            far,
            chunk,
        )
        sums.append((out[3], shifted(out[4], -2), shifted(out[5], -4)))
        dq_own.append(out[0])
        dq_other.append(swap(out[1]))
        norms.append(out[2])
        far_terms.append(out[6])

    strided_terms = exchanged(jnp.concatenate(far_terms, axis=1).reshape(pairs, 2, kv_width))
    parts = []
    for chunk, (own, near_terms, past_terms) in enumerate(sums):
        mine, theirs = collect(own, near_terms, past_terms, strided_terms, chunk)
        parts += [mine, swap(theirs)]
    grad_keys, grad_values = placed_grads(place, parts, half, kv_width)
    grad_queries = joined(jnp.concatenate(dq_own, axis=1), jnp.concatenate(dq_other, axis=1))
    norm = jnp.concatenate(norms, axis=0)
    log_norm = joined(norm[:, :half].T, swap(norm[:, half:]).T)
    return (grad_queries, grad_keys, grad_values, log_norm)


def solution(mesh):
    placed = P(("groups", "ctx"), "head")
    return jax.shard_map(
        local,
        mesh=mesh,
        in_specs=(placed,) * 4,
        out_specs=(placed,) * 4,
        check_vma=False,
    )
```

```python
import functools
import math

import jax
import jax.numpy as jnp
from jax import lax
from jax.experimental import pallas as pl
from jax.experimental.pallas import tpu as pltpu
from jax.sharding import PartitionSpec as P

HEAD_SIZE = 128
W = 512
STRIDE = 128
CHUNKS = 2

NEG_FILL = -1e30
SCALE = 1.0 / math.sqrt(HEAD_SIZE)


def vmem_shape(shape, dtype):
    return pltpu.VMEM(shape, dtype)


def in_hbm(*arrays):
    return [pltpu.with_memory_space_constraint(x, pltpu.HBM) for x in arrays]


def in_vmem(*arrays):
    return [pltpu.with_memory_space_constraint(x, pltpu.VMEM) for x in arrays]


def head_columns(which, width=HEAD_SIZE):
    return pl.ds(pl.multiple_of(which * width, width), width)


def pair_position():
    index = lax.axis_index("ctx")
    return index & 1, index >> 1


def dot_nt(left, right):
    return lax.dot_general(
        left, right, (((1,), (1,)), ((), ())), preferred_element_type=jnp.float32
    )


def dot_nn(left, right):
    return lax.dot_general(
        left, right, (((1,), (0,)), ((), ())), preferred_element_type=jnp.float32
    )


def dot_tn(left, right):
    return lax.dot_general(
        left, right, (((0,), (0,)), ((), ())), preferred_element_type=jnp.float32
    )


def attention_kernel(
    chunk,
    q_own,
    q_other,
    o_own,
    o_other,
    kv_here_in,
    kv_near,
    kv_past,
    kv_far,
    dq_own,
    dq_other,
    norm,
    g_here,
    g_near,
    g_past,
    g_far,
    q_held,
    o_held,
    here_held,
    here_done,
    held_done,
):
    half = q_own.shape[0]
    rows = 2 * half
    far_rows = kv_far.shape[0]
    both = 2 * HEAD_SIZE
    count = kv_near.shape[1] // both
    width = dq_own.shape[1]
    heads = width // (count * HEAD_SIZE)
    core, pair = pair_position()
    here = here_held
    loads = []
    for at in range(count):
        columns = slice(at * both, (at + 1) * both)
        first = core * (count * CHUNKS) + chunk * count + at
        for side in range(2):
            batch = []
            if side == 0:
                batch.append(
                    pltpu.make_async_copy(
                        kv_here_in.at[:, columns], here_held.at[:, columns], here_done.at[at]
                    )
                )
            for which in range(2):
                source = (q_own, q_other, o_own, o_other)[2 * which + side]
                batch.append(
                    pltpu.make_async_copy(
                        source.at[:, head_columns(first, heads * HEAD_SIZE)],
                        (q_held, o_held)[which].at[at, side],
                        held_done.at[at, side, which],
                    )
                )
            loads.append(batch)
    for copy in sum(loads, []):
        copy.start()
    wide = (half, rows)
    lane = lax.broadcasted_iota(jnp.int32, wide, 1) % half
    lower = lax.broadcasted_iota(jnp.int32, wide, 0) <= lane
    far_at = lax.broadcasted_iota(jnp.int32, (far_rows, rows), 0)
    far_lane = lax.broadcasted_iota(jnp.int32, (far_rows, rows), 1) % half
    far_token = far_at * half
    near_bias = jnp.where(pair >= 1, 0.0, NEG_FILL)
    past_bias = jnp.where(pair >= 2, 0.0, NEG_FILL)
    sides = []
    for side in range(2):
        later = core if side == 0 else 1 - core
        sides.append(
            (
                later,
                far_token <= pair * rows + later * half + far_lane - W,
                jnp.where(later == 0, past_bias, 0.0),
            )
        )

    def keys_of(at, side, which):
        columns = slice((2 * at + which) * HEAD_SIZE, (2 * at + which + 1) * HEAD_SIZE)
        far_row = 2 * (chunk * count + at) + which
        same = slice(side * half, (side + 1) * half)
        cross = slice((1 - side) * half, (2 - side) * half)
        full = jnp.where(sides[side][0] == 1, here[cross, columns], kv_past[cross, columns])
        return jnp.concatenate(
            [
                here[same, columns],
                kv_past[same, columns],
                full,
                kv_near[:, columns],
                kv_far[:, far_row, :],
            ],
            axis=0,
        )

    def operands(at, side, first):
        query, grad = (
            jnp.concatenate(
                [
                    held[at, side, :, (first + k) * HEAD_SIZE : (first + k + 1) * HEAD_SIZE]
                    for k in range(2)
                ],
                axis=0,
            )
            for held in (q_held, o_held)
        )
        key_all, value_all = keys_of(at, side, 0), keys_of(at, side, 1)
        return query, grad, key_all, dot_nt(key_all, query), dot_nt(value_all, grad)

    def merged(whole, bias):
        edge = jnp.where(lower, whole[:half], whole[half:rows] + bias)
        return edge, whole[rows : rows + half], whole[rows + half : 2 * rows + half]

    def reduced(op, parts):
        out = [op(part, axis=0, keepdims=True) for part in parts]
        return out

    def weights(at, side, first, score, dprob):
        _, far_open, full_bias = sides[side]
        edge, full, near = merged(score, past_bias)
        parts = [
            edge,
            full + full_bias,
            near + near_bias,
            jnp.where(far_open, score[2 * rows + half :], NEG_FILL),
        ]
        top = functools.reduce(jnp.maximum, reduced(jnp.max, parts))
        parts = [jnp.exp2((part - top) * (SCALE * math.log2(math.e))) for part in parts]
        total = sum(reduced(jnp.sum, parts))
        log_total = top * SCALE + jnp.log(total)
        for k in range(2):
            row = at * heads + first + k
            norm[row : row + 1, side * half : (side + 1) * half] = log_total[
                :, k * half : (k + 1) * half
            ]
        inverse = 1.0 / total
        parts = [part * inverse for part in parts]
        d_parts = [*merged(dprob, 0.0), dprob[2 * rows + half :]]
        delta = sum(reduced(jnp.sum, [part * d_part for part, d_part in zip(parts, d_parts)]))
        d_parts = [part * (d_part - delta) for part, d_part in zip(parts, d_parts)]

        def split(edge, *others):
            return jnp.concatenate(
                [
                    jnp.where(lower, edge, 0.0).astype(jnp.bfloat16),
                    jnp.where(lower, 0.0, edge).astype(jnp.bfloat16),
                    *(part.astype(jnp.bfloat16) for part in others),
                ],
                axis=0,
            )

        return split(*parts), split(*d_parts)

    steps = [
        (at, side, first)
        for at in range(count)
        for side in range(2)
        for first in range(0, heads, 2)
    ]
    for copy in sum(loads, []):
        copy.wait()
    following = operands(*steps[0])
    terms = {}
    for number, (at, side, first) in enumerate(steps):
        query, grad, key_all, score, dprob = following
        if number + 1 < len(steps):
            following = operands(*steps[number + 1])
        prob, dscore = weights(at, side, first, score, dprob)
        new = (dot_nn(dscore, query), dot_nn(prob, grad))
        terms[side] = new if first == 0 else tuple(a + b for a, b in zip(terms[side], new))
        query_term = (dot_tn(key_all, dscore) * SCALE).T.astype(jnp.bfloat16)
        dq_side = dq_own if side == 0 else dq_other
        for k in range(2):
            columns = slice(
                (at * heads + first + k) * HEAD_SIZE, (at * heads + first + k + 1) * HEAD_SIZE
            )
            dq_side[:, columns] = query_term[k * half : (k + 1) * half]
        if side == 1 and first + 2 == heads:
            for which in range(2):
                scale = SCALE if which == 0 else 1.0
                columns = slice((2 * at + which) * HEAD_SIZE, (2 * at + which + 1) * HEAD_SIZE)
                own, other = (terms[k][which] * scale for k in range(2))
                for k, (mine, theirs) in enumerate(((own, other), (other, own))):
                    cross = theirs[rows : rows + half]
                    here_too = sides[1 - k][0] == 1
                    place = slice(k * half, (k + 1) * half)
                    g_here[place, columns] = mine[:half] + jnp.where(here_too, cross, 0.0)
                    g_past[place, columns] = (
                        mine[half:rows] + jnp.where(here_too, 0.0, cross)
                    ).astype(jnp.bfloat16)
                joint = own[rows + half :] + other[rows + half :]
                g_near[:, columns] = joint[:rows].astype(jnp.bfloat16)
                g_far[:, columns] = joint[rows:]


def attention(queries, q_other, grad_out, o_other, kv_here, kv_near, kv_past, kv_far, chunk):
    half = queries.shape[0]
    rows = 2 * half
    far_rows = kv_far.shape[0]
    both = 2 * HEAD_SIZE
    count = kv_here.shape[1] // both
    per_core = count * CHUNKS
    group_width = queries.shape[1] // (2 * per_core)
    heads = group_width // HEAD_SIZE

    whole = pl.BlockSpec(memory_space=pltpu.VMEM)
    keys_seen = 3 * rows + far_rows
    return pl.pallas_call(
        functools.partial(attention_kernel, chunk),
        name=f"attention_{chunk}",
        in_specs=[pl.BlockSpec(memory_space=pl.ANY)] * 5 + [whole] * 3,
        out_specs=[whole] * 7,
        out_shape=[
            vmem_shape((half, count * group_width), jnp.bfloat16),
            vmem_shape((half, count * group_width), jnp.bfloat16),
            vmem_shape((count * heads, rows), jnp.float32),
            vmem_shape((rows, count * both), jnp.float32),
            vmem_shape((rows, count * both), jnp.bfloat16),
            vmem_shape((rows, count * both), jnp.bfloat16),
            vmem_shape((far_rows, count * both), jnp.float32),
        ],
        scratch_shapes=[
            pltpu.VMEM((count, 2, half, group_width), jnp.bfloat16),
            pltpu.VMEM((count, 2, half, group_width), jnp.bfloat16),
            pltpu.VMEM((rows, count * both), jnp.bfloat16),
            pltpu.SemaphoreType.DMA((count,)),
            pltpu.SemaphoreType.DMA((count, 2, 2)),
        ],
        compiler_params=pltpu.CompilerParams(vmem_limit_bytes=20 * 1024 * 1024),
        cost_estimate=pl.CostEstimate(
            flops=count * heads * rows * keys_seen * HEAD_SIZE * 20,
            transcendentals=count * heads * rows * keys_seen,
            bytes_accessed=count * (6 * half * group_width * 2 + 5 * rows * both * 4),
        ),
    )(
        *in_hbm(queries, q_other, grad_out, o_other, kv_here), *in_vmem(kv_near, kv_past, kv_far)
    )


def arrange_kernel(keys, values, k_other, v_other, *outs):
    half = keys.shape[0]
    payloads = outs
    core, _ = pair_position()
    count = payloads[0].shape[1] // (2 * HEAD_SIZE)
    for chunk, payload in enumerate(payloads):
        for h in range(count):
            source = head_columns(core * (count * CHUNKS) + chunk * count + h)
            for side, (mine, theirs) in enumerate(((keys, k_other), (values, v_other))):
                to = slice((2 * h + side) * HEAD_SIZE, (2 * h + side + 1) * HEAD_SIZE)
                payload[:half, to] = mine[:, source]
                payload[half:, to] = theirs[:, source]


def own_rows_kernel(keys, values, out):
    per_core = out.shape[1] // 2
    for core in range(2):
        rows = []
        for h in range(core * per_core, (core + 1) * per_core):
            columns = slice(h * HEAD_SIZE, (h + 1) * HEAD_SIZE)
            rows += [keys[0:1, columns], values[0:1, columns]]
        block = jnp.concatenate([row.astype(jnp.float32) for row in rows], axis=0)
        for peer in range(core, out.shape[0], 2):
            out[peer] = block.astype(out.dtype)


def own_rows(keys, values, peers):
    kv_width = keys.shape[1]
    head = pl.BlockSpec((16, kv_width), lambda i: (0, 0))
    shape = (peers, kv_width // HEAD_SIZE, HEAD_SIZE)
    return pl.pallas_call(
        own_rows_kernel,
        name="own_rows",
        grid=(1,),
        in_specs=[head, head],
        out_specs=pl.BlockSpec(shape, lambda i: (0, 0, 0)),
        out_shape=jax.ShapeDtypeStruct(shape, keys.dtype),
    )(keys, values)


def arrange(keys, values, k_other, v_other):
    half, kv_width = keys.shape
    whole = pl.BlockSpec(memory_space=pltpu.VMEM)
    payload = pltpu.HBM((2 * half, kv_width // CHUNKS), keys.dtype)
    return pl.pallas_call(
        arrange_kernel,
        name="arrange",
        grid=(1,),
        in_specs=[pl.BlockSpec(keys.shape, lambda i: (0, 0))] * 2 + [whole] * 2,
        out_specs=[whole] * CHUNKS,
        out_shape=[payload] * CHUNKS,
    )(keys, values, *in_vmem(k_other, v_other))


def collect_kernel(chunk, here, near, past, strided, mine, theirs):
    half, width = mine.shape
    core, _ = pair_position()
    extra = jnp.sum(strided[:, :, chunk * width : (chunk + 1) * width], axis=0)
    extra = jnp.where(core == 0, extra, jnp.concatenate([extra[1:2], extra[0:1]], axis=0))
    total = here[...] + near[...].astype(jnp.float32) + past[...].astype(jnp.float32)
    row = lax.broadcasted_iota(jnp.int32, (half, 1), 0)
    mine[...] = (total[:half] + jnp.where(row == 0, extra[0:1], 0.0)).astype(mine.dtype)
    theirs[...] = (total[half:] + jnp.where(row == 0, extra[1:2], 0.0)).astype(theirs.dtype)


def collect(here, near, past, strided, chunk):
    rows, width = here.shape
    half = vmem_shape((rows // 2, width), jnp.bfloat16)
    whole = pl.BlockSpec(memory_space=pltpu.VMEM)
    return pl.pallas_call(
        functools.partial(collect_kernel, chunk),
        name=f"collect_{chunk}",
        in_specs=[whole] * 4,
        out_specs=[whole, whole],
        out_shape=[half, half],
        cost_estimate=pl.CostEstimate(
            flops=rows * width * 4, transcendentals=0, bytes_accessed=rows * width * 10
        ),
    )(*in_vmem(here, near, past, strided))


def place_kernel(*refs):
    here, _ = pair_position()
    *parts, grad_keys, grad_values = refs
    count = parts[0].shape[1] // (2 * HEAD_SIZE)
    for chunk in range(CHUNKS):
        mine, theirs = parts[2 * chunk : 2 * chunk + 2]
        for h in range(count):
            at = chunk * count + h
            for core, block in ((here, mine), (1 - here, theirs)):
                to = head_columns(core * (count * CHUNKS) + at)
                grad_keys[:, to] = block[:, 2 * h * HEAD_SIZE : (2 * h + 1) * HEAD_SIZE]
                grad_values[:, to] = block[:, (2 * h + 1) * HEAD_SIZE : (2 * h + 2) * HEAD_SIZE]


def placed_grads(parts, half, kv_width):
    whole = pl.BlockSpec(memory_space=pltpu.VMEM)
    out = jax.ShapeDtypeStruct((half, kv_width), jnp.bfloat16)
    return pl.pallas_call(
        place_kernel,
        name="place",
        in_specs=[whole] * len(parts),
        out_specs=[whole, whole],
        out_shape=[out, out],
    )(*in_vmem(*parts))


def local(queries, keys, values, grad_out):
    half, kv_width = keys.shape
    kv_heads = kv_width // HEAD_SIZE
    rows = 2 * half
    peers = lax.axis_size("ctx")
    pairs = peers // 2
    assert half == STRIDE and W == 2 * rows and peers % 2 == 0 and kv_heads % (2 * CHUNKS) == 0
    core, _ = pair_position()

    def swap(x):
        return lax.ppermute(x, "ctx", [(i, i ^ 1) for i in range(peers)])

    def shifted(x, by):
        return lax.ppermute(x, "ctx", [(i, (i + by) % peers) for i in range(peers)])

    def exchanged(x):
        groups = [list(range(parity, peers, 2)) for parity in range(2)]
        return lax.all_to_all(x, "ctx", 0, 0, axis_index_groups=groups)

    def joined(mine, theirs):
        return jnp.where(
            core == 0,
            jnp.concatenate([mine, theirs], axis=1),
            jnp.concatenate([theirs, mine], axis=1),
        )

    far = lax.all_to_all(own_rows(keys, values, peers), "ctx", 0, 0, tiled=True)
    here = arrange(keys, values, swap(keys), swap(values))
    near, past = [], []
    for chunk in range(CHUNKS):
        payload = here[chunk]
        if chunk > 0:
            payload, _ = lax.optimization_barrier((payload, far))
        near.append(shifted(payload, 2))
        past.append(shifted(payload, 4))
    q_sent, o_sent, _ = lax.optimization_barrier((queries, grad_out, here[0]))
    q_other, o_other = swap(q_sent), swap(o_sent)

    dq_own, dq_other, norms, sums, far_terms = [], [], [], [], []
    for chunk in range(CHUNKS):
        out = attention(
            queries,
            q_other,
            grad_out,
            o_other,
            here[chunk],
            near[chunk],
            past[chunk],
            far,
            chunk,
        )
        sums.append((out[3], shifted(out[4], -2), shifted(out[5], -4)))
        dq_own.append(out[0])
        dq_other.append(swap(out[1]))
        norms.append(out[2])
        far, _ = lax.optimization_barrier((far, out[2]))
        far_terms.append(out[6])

    strided_terms = exchanged(jnp.concatenate(far_terms, axis=1).reshape(pairs, 2, kv_width))
    grad_queries = joined(jnp.concatenate(dq_own, axis=1), jnp.concatenate(dq_other, axis=1))
    norm = jnp.concatenate(norms, axis=0)
    log_norm = joined(norm[:, :half].T, swap(norm[:, half:]).T)
    parts = []
    for chunk, (own, near_terms, past_terms) in enumerate(sums):
        if chunk > 0:
            own, grad_queries, log_norm, _ = lax.optimization_barrier(
                (own, grad_queries, log_norm, parts[-2])
            )
        mine, theirs = collect(own, near_terms, past_terms, strided_terms, chunk)
        parts += [mine, swap(theirs)]
    grad_keys, grad_values = placed_grads(parts, half, kv_width)
    return (grad_queries, grad_keys, grad_values, log_norm)


def solution(mesh):
    placed = P(("groups", "ctx"), "head")
    return jax.shard_map(
        local,
        mesh=mesh,
        in_specs=(placed,) * 4,
        out_specs=(placed,) * 4,
        check_vma=False,
    )
```

```python
import functools
import math

import jax
import jax.numpy as jnp
from jax import lax
from jax.experimental import pallas as pl
from jax.experimental.pallas import tpu as pltpu
from jax.sharding import PartitionSpec as P

HEAD_SIZE = 128
W = 512
STRIDE = 128
CHUNKS = 2

NEG_FILL = -1e30
SCALE = 1.0 / math.sqrt(HEAD_SIZE)


def vmem_shape(shape, dtype):
    return pltpu.VMEM(shape, dtype)


def in_hbm(*arrays):
    return [pltpu.with_memory_space_constraint(x, pltpu.HBM) for x in arrays]


def in_vmem(*arrays):
    return [pltpu.with_memory_space_constraint(x, pltpu.VMEM) for x in arrays]


def head_columns(which, width=HEAD_SIZE):
    return pl.ds(pl.multiple_of(which * width, width), width)


def pair_position():
    index = lax.axis_index("ctx")
    return index & 1, index >> 1


def dot_nt(left, right):
    return lax.dot_general(
        left, right, (((1,), (1,)), ((), ())), preferred_element_type=jnp.float32
    )


def dot_nn(left, right):
    return lax.dot_general(
        left, right, (((1,), (0,)), ((), ())), preferred_element_type=jnp.float32
    )


def dot_tn(left, right):
    return lax.dot_general(
        left, right, (((0,), (0,)), ((), ())), preferred_element_type=jnp.float32
    )


def attention_kernel(
    chunk,
    q_own,
    q_other,
    o_own,
    o_other,
    kv_here_in,
    kv_near,
    kv_past,
    kv_far,
    dq_own,
    dq_other,
    norm,
    g_here,
    g_near,
    g_past,
    g_far,
    q_held,
    o_held,
    here_held,
    here_done,
    held_done,
):
    half = q_own.shape[0]
    rows = 2 * half
    far_rows = kv_far.shape[0]
    both = 2 * HEAD_SIZE
    count = kv_near.shape[1] // both
    width = dq_own.shape[1]
    heads = width // (count * HEAD_SIZE)
    core, pair = pair_position()
    here = here_held
    loads = []
    for at in range(count):
        columns = slice(at * both, (at + 1) * both)
        first = core * (count * CHUNKS) + chunk * count + at
        for side in range(2):
            batch = []
            if side == 0:
                batch.append(
                    pltpu.make_async_copy(
                        kv_here_in.at[:, columns], here_held.at[:, columns], here_done.at[at]
                    )
                )
            for which in range(2):
                source = (q_own, q_other, o_own, o_other)[2 * which + side]
                batch.append(
                    pltpu.make_async_copy(
                        source.at[:, head_columns(first, heads * HEAD_SIZE)],
                        (q_held, o_held)[which].at[at, side],
                        held_done.at[at, side, which],
                    )
                )
            loads.append(batch)
    for copy in sum(loads, []):
        copy.start()
    wide = (half, rows)
    lane = lax.broadcasted_iota(jnp.int32, wide, 1) % half
    lower = lax.broadcasted_iota(jnp.int32, wide, 0) <= lane
    far_at = lax.broadcasted_iota(jnp.int32, (far_rows, rows), 0)
    far_lane = lax.broadcasted_iota(jnp.int32, (far_rows, rows), 1) % half
    far_token = far_at * half
    near_bias = jnp.where(pair >= 1, 0.0, NEG_FILL)
    past_bias = jnp.where(pair >= 2, 0.0, NEG_FILL)
    sides = []
    for side in range(2):
        later = core if side == 0 else 1 - core
        sides.append(
            (
                later,
                far_token <= pair * rows + later * half + far_lane - W,
                jnp.where(later == 0, past_bias, 0.0),
            )
        )

    def keys_of(at, side, which):
        columns = slice((2 * at + which) * HEAD_SIZE, (2 * at + which + 1) * HEAD_SIZE)
        far_row = 2 * (chunk * count + at) + which
        same = slice(side * half, (side + 1) * half)
        cross = slice((1 - side) * half, (2 - side) * half)
        full = jnp.where(sides[side][0] == 1, here[cross, columns], kv_past[cross, columns])
        return jnp.concatenate(
            [
                here[same, columns],
                kv_past[same, columns],
                full,
                kv_near[:, columns],
                kv_far[:, far_row, :],
            ],
            axis=0,
        )

    def operands(at, side, first):
        query, grad = (
            jnp.concatenate(
                [
                    held[at, side, :, (first + k) * HEAD_SIZE : (first + k + 1) * HEAD_SIZE]
                    for k in range(2)
                ],
                axis=0,
            )
            for held in (q_held, o_held)
        )
        key_all, value_all = keys_of(at, side, 0), keys_of(at, side, 1)
        return query, grad, key_all, dot_nt(key_all, query), dot_nt(value_all, grad)

    def merged(whole, bias):
        edge = jnp.where(lower, whole[:half], whole[half:rows] + bias)
        return edge, whole[rows : rows + half], whole[rows + half : 2 * rows + half]

    def reduced(op, parts):
        out = [op(part, axis=0, keepdims=True) for part in parts]
        return out

    def weights(at, side, first, score, dprob):
        _, far_open, full_bias = sides[side]
        edge, full, near = merged(score, past_bias)
        parts = [
            edge,
            full + full_bias,
            near + near_bias,
            jnp.where(far_open, score[2 * rows + half :], NEG_FILL),
        ]
        top = functools.reduce(jnp.maximum, reduced(jnp.max, parts))
        parts = [jnp.exp2((part - top) * (SCALE * math.log2(math.e))) for part in parts]
        total = sum(reduced(jnp.sum, parts))
        log_total = top * SCALE + jnp.log(total)
        for k in range(2):
            row = at * heads + first + k
            norm[row : row + 1, side * half : (side + 1) * half] = log_total[
                :, k * half : (k + 1) * half
            ]
        inverse = 1.0 / total
        parts = [part * inverse for part in parts]
        d_parts = [*merged(dprob, 0.0), dprob[2 * rows + half :]]
        delta = sum(reduced(jnp.sum, [part * d_part for part, d_part in zip(parts, d_parts)]))
        d_parts = [part * (d_part - delta) for part, d_part in zip(parts, d_parts)]

        def split(edge, *others):
            return jnp.concatenate(
                [
                    jnp.where(lower, edge, 0.0).astype(jnp.bfloat16),
                    jnp.where(lower, 0.0, edge).astype(jnp.bfloat16),
                    *(part.astype(jnp.bfloat16) for part in others),
                ],
                axis=0,
            )

        return split(*parts), split(*d_parts)

    steps = [
        (at, side, first)
        for at in range(count)
        for side in range(2)
        for first in range(0, heads, 2)
    ]
    for copy in sum(loads, []):
        copy.wait()
    following = operands(*steps[0])
    terms = {}
    for number, (at, side, first) in enumerate(steps):
        query, grad, key_all, score, dprob = following
        if number + 1 < len(steps):
            following = operands(*steps[number + 1])
        prob, dscore = weights(at, side, first, score, dprob)
        new = (dot_nn(dscore, query), dot_nn(prob, grad))
        terms[side] = new if first == 0 else tuple(a + b for a, b in zip(terms[side], new))
        query_term = (dot_tn(key_all, dscore) * SCALE).T.astype(jnp.bfloat16)
        dq_side = dq_own if side == 0 else dq_other
        for k in range(2):
            columns = slice(
                (at * heads + first + k) * HEAD_SIZE, (at * heads + first + k + 1) * HEAD_SIZE
            )
            dq_side[:, columns] = query_term[k * half : (k + 1) * half]
        if side == 1 and first + 2 == heads:
            for which in range(2):
                scale = SCALE if which == 0 else 1.0
                columns = slice((2 * at + which) * HEAD_SIZE, (2 * at + which + 1) * HEAD_SIZE)
                own, other = (terms[k][which] * scale for k in range(2))
                for k, (mine, theirs) in enumerate(((own, other), (other, own))):
                    cross = theirs[rows : rows + half]
                    here_too = sides[1 - k][0] == 1
                    place = slice(k * half, (k + 1) * half)
                    g_here[place, columns] = mine[:half] + jnp.where(here_too, cross, 0.0)
                    g_past[place, columns] = (
                        mine[half:rows] + jnp.where(here_too, 0.0, cross)
                    ).astype(jnp.bfloat16)
                joint = own[rows + half :] + other[rows + half :]
                g_near[:, columns] = joint[:rows].astype(jnp.bfloat16)
                g_far[:, columns] = joint[rows:]


def attention(queries, q_other, grad_out, o_other, kv_here, kv_near, kv_past, kv_far, chunk):
    half = queries.shape[0]
    rows = 2 * half
    far_rows = kv_far.shape[0]
    both = 2 * HEAD_SIZE
    count = kv_here.shape[1] // both
    per_core = count * CHUNKS
    group_width = queries.shape[1] // (2 * per_core)
    heads = group_width // HEAD_SIZE

    whole = pl.BlockSpec(memory_space=pltpu.VMEM)
    keys_seen = 3 * rows + far_rows
    return pl.pallas_call(
        functools.partial(attention_kernel, chunk),
        name=f"attention_{chunk}",
        in_specs=[pl.BlockSpec(memory_space=pl.ANY)] * 5 + [whole] * 3,
        out_specs=[whole] * 7,
        out_shape=[
            vmem_shape((half, count * group_width), jnp.bfloat16),
            vmem_shape((half, count * group_width), jnp.bfloat16),
            vmem_shape((count * heads, rows), jnp.float32),
            vmem_shape((rows, count * both), jnp.float32),
            vmem_shape((rows, count * both), jnp.bfloat16),
            vmem_shape((rows, count * both), jnp.bfloat16),
            vmem_shape((far_rows, count * both), jnp.float32),
        ],
        scratch_shapes=[
            pltpu.VMEM((count, 2, half, group_width), jnp.bfloat16),
            pltpu.VMEM((count, 2, half, group_width), jnp.bfloat16),
            pltpu.VMEM((rows, count * both), jnp.bfloat16),
            pltpu.SemaphoreType.DMA((count,)),
            pltpu.SemaphoreType.DMA((count, 2, 2)),
        ],
        compiler_params=pltpu.CompilerParams(vmem_limit_bytes=20 * 1024 * 1024),
        cost_estimate=pl.CostEstimate(
            flops=count * heads * rows * keys_seen * HEAD_SIZE * 20,
            transcendentals=count * heads * rows * keys_seen,
            bytes_accessed=count * (6 * half * group_width * 2 + 5 * rows * both * 4),
        ),
    )(
        *in_hbm(queries, q_other, grad_out, o_other, kv_here), *in_vmem(kv_near, kv_past, kv_far)
    )


def arrange_kernel(chunk, keys, values, k_other, v_other, payload):
    half = keys.shape[0]
    core, _ = pair_position()
    count = payload.shape[1] // (2 * HEAD_SIZE)
    for h in range(count):
        source = head_columns(core * (count * CHUNKS) + chunk * count + h)
        for side, (mine, theirs) in enumerate(((keys, k_other), (values, v_other))):
            to = slice((2 * h + side) * HEAD_SIZE, (2 * h + side + 1) * HEAD_SIZE)
            payload[:half, to] = mine[:, source]
            payload[half:, to] = theirs[:, source]


def arrange(keys, values, k_other, v_other, chunk):
    half, kv_width = keys.shape
    whole = pl.BlockSpec(memory_space=pltpu.VMEM)
    return pl.pallas_call(
        functools.partial(arrange_kernel, chunk),
        name=f"arrange_{chunk}",
        grid=(1,),
        in_specs=[pl.BlockSpec(keys.shape, lambda i: (0, 0))] * 2 + [whole] * 2,
        out_specs=whole,
        out_shape=pltpu.HBM((2 * half, kv_width // CHUNKS), keys.dtype),
    )(keys, values, *in_vmem(k_other, v_other))


def own_rows_kernel(keys, values, out):
    per_core = out.shape[1] // 2
    for core in range(2):
        rows = []
        for h in range(core * per_core, (core + 1) * per_core):
            columns = slice(h * HEAD_SIZE, (h + 1) * HEAD_SIZE)
            rows += [keys[0:1, columns], values[0:1, columns]]
        block = jnp.concatenate([row.astype(jnp.float32) for row in rows], axis=0)
        for peer in range(core, out.shape[0], 2):
            out[peer] = block.astype(out.dtype)


def own_rows(keys, values, peers):
    kv_width = keys.shape[1]
    head = pl.BlockSpec((16, kv_width), lambda i: (0, 0))
    shape = (peers, kv_width // HEAD_SIZE, HEAD_SIZE)
    return pl.pallas_call(
        own_rows_kernel,
        name="own_rows",
        grid=(1,),
        in_specs=[head, head],
        out_specs=pl.BlockSpec(shape, lambda i: (0, 0, 0)),
        out_shape=jax.ShapeDtypeStruct(shape, keys.dtype),
    )(keys, values)


def collect_kernel(chunk, here, near, past, strided, mine, theirs):
    half, width = mine.shape
    core, _ = pair_position()
    extra = jnp.sum(strided[:, :, chunk * width : (chunk + 1) * width], axis=0)
    extra = jnp.where(core == 0, extra, jnp.concatenate([extra[1:2], extra[0:1]], axis=0))
    total = here[...] + near[...].astype(jnp.float32) + past[...].astype(jnp.float32)
    row = lax.broadcasted_iota(jnp.int32, (half, 1), 0)
    mine[...] = (total[:half] + jnp.where(row == 0, extra[0:1], 0.0)).astype(mine.dtype)
    theirs[...] = (total[half:] + jnp.where(row == 0, extra[1:2], 0.0)).astype(theirs.dtype)


def collect(here, near, past, strided, chunk):
    rows, width = here.shape
    half = vmem_shape((rows // 2, width), jnp.bfloat16)
    whole = pl.BlockSpec(memory_space=pltpu.VMEM)
    return pl.pallas_call(
        functools.partial(collect_kernel, chunk),
        name=f"collect_{chunk}",
        in_specs=[whole] * 4,
        out_specs=[whole, whole],
        out_shape=[half, half],
        cost_estimate=pl.CostEstimate(
            flops=rows * width * 4, transcendentals=0, bytes_accessed=rows * width * 10
        ),
    )(*in_vmem(here, near, past, strided))


def place_kernel(*refs):
    here, _ = pair_position()
    *parts, grad_keys, grad_values = refs
    count = parts[0].shape[1] // (2 * HEAD_SIZE)
    for chunk in range(CHUNKS):
        mine, theirs = parts[2 * chunk : 2 * chunk + 2]
        for h in range(count):
            at = chunk * count + h
            for core, block in ((here, mine), (1 - here, theirs)):
                to = head_columns(core * (count * CHUNKS) + at)
                grad_keys[:, to] = block[:, 2 * h * HEAD_SIZE : (2 * h + 1) * HEAD_SIZE]
                grad_values[:, to] = block[:, (2 * h + 1) * HEAD_SIZE : (2 * h + 2) * HEAD_SIZE]


def placed_grads(parts, half, kv_width):
    whole = pl.BlockSpec(memory_space=pltpu.VMEM)
    out = jax.ShapeDtypeStruct((half, kv_width), jnp.bfloat16)
    return pl.pallas_call(
        place_kernel,
        name="place",
        in_specs=[whole] * len(parts),
        out_specs=[whole, whole],
        out_shape=[out, out],
    )(*in_vmem(*parts))


def local(queries, keys, values, grad_out):
    half, kv_width = keys.shape
    kv_heads = kv_width // HEAD_SIZE
    rows = 2 * half
    peers = lax.axis_size("ctx")
    pairs = peers // 2
    assert half == STRIDE and W == 2 * rows and peers % 2 == 0 and kv_heads % (2 * CHUNKS) == 0
    core, _ = pair_position()

    def swap(x):
        return lax.ppermute(x, "ctx", [(i, i ^ 1) for i in range(peers)])

    def shifted(x, by):
        return lax.ppermute(x, "ctx", [(i, (i + by) % peers) for i in range(peers)])

    def exchanged(x):
        groups = [list(range(parity, peers, 2)) for parity in range(2)]
        return lax.all_to_all(x, "ctx", 0, 0, axis_index_groups=groups)

    def joined(mine, theirs):
        return jnp.where(
            core == 0,
            jnp.concatenate([mine, theirs], axis=1),
            jnp.concatenate([theirs, mine], axis=1),
        )

    sent = own_rows(keys, values, peers)
    k_other, v_other, sent = lax.optimization_barrier((swap(keys), swap(values), sent))
    far = lax.all_to_all(sent, "ctx", 0, 0, tiled=True)
    here = [arrange(keys, values, k_other, v_other, chunk) for chunk in range(CHUNKS)]
    near, past = [], []
    for chunk in range(CHUNKS):
        payload = here[chunk]
        if chunk > 0:
            payload, _ = lax.optimization_barrier((payload, far))
        near.append(shifted(payload, 2))
        past.append(shifted(payload, 4))
    q_sent, o_sent, _ = lax.optimization_barrier((queries, grad_out, here[0]))
    q_other, o_other = swap(q_sent), swap(o_sent)

    dq_own, dq_other, norms, sums, far_terms = [], [], [], [], []
    for chunk in range(CHUNKS):
        out = attention(
            queries,
            q_other,
            grad_out,
            o_other,
            here[chunk],
            near[chunk],
            past[chunk],
            far,
            chunk,
        )
        sums.append((out[3], shifted(out[4], -2), shifted(out[5], -4)))
        dq_own.append(out[0])
        dq_other.append(swap(out[1]))
        norms.append(out[2])
        far, _ = lax.optimization_barrier((far, out[2]))
        far_terms.append(out[6])

    terms, *_ = lax.optimization_barrier((jnp.concatenate(far_terms, axis=1), *sums[0][1:]))
    strided_terms = exchanged(terms.reshape(pairs, 2, kv_width))
    grad_queries = joined(jnp.concatenate(dq_own, axis=1), jnp.concatenate(dq_other, axis=1))
    norm = jnp.concatenate(norms, axis=0)
    log_norm = joined(norm[:, :half].T, swap(norm[:, half:]).T)
    parts = []
    for chunk, (own, near_terms, past_terms) in enumerate(sums):
        if chunk > 0:
            own, grad_queries, log_norm, _ = lax.optimization_barrier(
                (own, grad_queries, log_norm, parts[-2])
            )
        mine, theirs = collect(own, near_terms, past_terms, strided_terms, chunk)
        parts += [mine, swap(theirs)]
    grad_keys, grad_values = placed_grads(parts, half, kv_width)
    return (grad_queries, grad_keys, grad_values, log_norm)


def solution(mesh):
    placed = P(("groups", "ctx"), "head")
    return jax.shard_map(
        local,
        mesh=mesh,
        in_specs=(placed,) * 4,
        out_specs=(placed,) * 4,
        check_vma=False,
    )
```

```python
import functools
import math

import jax
import jax.numpy as jnp
from jax import lax
from jax.experimental import pallas as pl
from jax.experimental.pallas import tpu as pltpu
from jax.sharding import PartitionSpec as P

HEAD_SIZE = 128
W = 512
STRIDE = 128
CHUNKS = 2

NEG_FILL = -1e30
SCALE = 1.0 / math.sqrt(HEAD_SIZE)


def vmem_shape(shape, dtype):
    return pltpu.VMEM(shape, dtype)


def in_hbm(*arrays):
    return [pltpu.with_memory_space_constraint(x, pltpu.HBM) for x in arrays]


def in_vmem(*arrays):
    return [pltpu.with_memory_space_constraint(x, pltpu.VMEM) for x in arrays]


def head_columns(which, width=HEAD_SIZE):
    return pl.ds(pl.multiple_of(which * width, width), width)


def pair_position():
    index = lax.axis_index("ctx")
    return index & 1, index >> 1


def dot_nt(left, right):
    return lax.dot_general(
        left, right, (((1,), (1,)), ((), ())), preferred_element_type=jnp.float32
    )


def dot_nn(left, right):
    return lax.dot_general(
        left, right, (((1,), (0,)), ((), ())), preferred_element_type=jnp.float32
    )


def dot_tn(left, right):
    return lax.dot_general(
        left, right, (((0,), (0,)), ((), ())), preferred_element_type=jnp.float32
    )


def attention_kernel(
    chunk,
    q_own,
    q_other,
    o_own,
    o_other,
    kv_here_in,
    kv_near,
    kv_past,
    kv_far,
    dq_own,
    dq_other,
    norm,
    g_here,
    g_near,
    g_past,
    g_far,
    q_held,
    o_held,
    here_held,
    here_done,
    held_done,
):
    half = q_own.shape[0]
    rows = 2 * half
    far_rows = kv_far.shape[0]
    both = 2 * HEAD_SIZE
    count = kv_near.shape[1] // both
    width = dq_own.shape[1]
    heads = width // (count * HEAD_SIZE)
    core, pair = pair_position()
    here = here_held
    loads = []
    for at in range(count):
        columns = slice(at * both, (at + 1) * both)
        first = core * (count * CHUNKS) + chunk * count + at
        for side in range(2):
            batch = []
            if side == 0:
                batch.append(
                    pltpu.make_async_copy(
                        kv_here_in.at[:, columns], here_held.at[:, columns], here_done.at[at]
                    )
                )
            for which in range(2):
                source = (q_own, q_other, o_own, o_other)[2 * which + side]
                batch.append(
                    pltpu.make_async_copy(
                        source.at[:, head_columns(first, heads * HEAD_SIZE)],
                        (q_held, o_held)[which].at[at, side],
                        held_done.at[at, side, which],
                    )
                )
            loads.append(batch)
    for copy in sum(loads, []):
        copy.start()
    wide = (half, rows)
    lane = lax.broadcasted_iota(jnp.int32, wide, 1) % half
    lower = lax.broadcasted_iota(jnp.int32, wide, 0) <= lane
    far_at = lax.broadcasted_iota(jnp.int32, (far_rows, rows), 0)
    far_lane = lax.broadcasted_iota(jnp.int32, (far_rows, rows), 1) % half
    far_token = far_at * half
    near_bias = jnp.where(pair >= 1, 0.0, NEG_FILL)
    past_bias = jnp.where(pair >= 2, 0.0, NEG_FILL)
    sides = []
    for side in range(2):
        later = core if side == 0 else 1 - core
        sides.append(
            (
                later,
                far_token <= pair * rows + later * half + far_lane - W,
                jnp.where(later == 0, past_bias, 0.0),
            )
        )

    def keys_of(at, side, which):
        columns = slice((2 * at + which) * HEAD_SIZE, (2 * at + which + 1) * HEAD_SIZE)
        far_row = 2 * (chunk * count + at) + which
        same = slice(side * half, (side + 1) * half)
        cross = slice((1 - side) * half, (2 - side) * half)
        full = jnp.where(sides[side][0] == 1, here[cross, columns], kv_past[cross, columns])
        return jnp.concatenate(
            [
                here[same, columns],
                kv_past[same, columns],
                full,
                kv_near[:, columns],
                kv_far[:, far_row, :],
            ],
            axis=0,
        )

    def operands(at, side, first):
        query, grad = (
            jnp.concatenate(
                [
                    held[at, side, :, (first + k) * HEAD_SIZE : (first + k + 1) * HEAD_SIZE]
                    for k in range(2)
                ],
                axis=0,
            )
            for held in (q_held, o_held)
        )
        key_all, value_all = keys_of(at, side, 0), keys_of(at, side, 1)
        return query, grad, key_all, dot_nt(key_all, query), dot_nt(value_all, grad)

    def merged(whole, bias):
        edge = jnp.where(lower, whole[:half], whole[half:rows] + bias)
        return edge, whole[rows : rows + half], whole[rows + half : 2 * rows + half]

    def reduced(op, parts):
        out = [op(part, axis=0, keepdims=True) for part in parts]
        return out

    def weights(at, side, first, score, dprob):
        _, far_open, full_bias = sides[side]
        edge, full, near = merged(score, past_bias)
        parts = [
            edge,
            full + full_bias,
            near + near_bias,
            jnp.where(far_open, score[2 * rows + half :], NEG_FILL),
        ]
        top = functools.reduce(jnp.maximum, reduced(jnp.max, parts))
        parts = [jnp.exp2((part - top) * (SCALE * math.log2(math.e))) for part in parts]
        total = sum(reduced(jnp.sum, parts))
        log_total = top * SCALE + jnp.log(total)
        for k in range(2):
            row = at * heads + first + k
            norm[row : row + 1, side * half : (side + 1) * half] = log_total[
                :, k * half : (k + 1) * half
            ]
        inverse = 1.0 / total
        parts = [part * inverse for part in parts]
        d_parts = [*merged(dprob, 0.0), dprob[2 * rows + half :]]
        delta = sum(reduced(jnp.sum, [part * d_part for part, d_part in zip(parts, d_parts)]))
        d_parts = [part * (d_part - delta) for part, d_part in zip(parts, d_parts)]

        def split(edge, *others):
            return jnp.concatenate(
                [
                    jnp.where(lower, edge, 0.0).astype(jnp.bfloat16),
                    jnp.where(lower, 0.0, edge).astype(jnp.bfloat16),
                    *(part.astype(jnp.bfloat16) for part in others),
                ],
                axis=0,
            )

        return split(*parts), split(*d_parts)

    steps = [
        (at, side, first)
        for at in range(count)
        for side in range(2)
        for first in range(0, heads, 2)
    ]
    for copy in sum(loads, []):
        copy.wait()
    following = operands(*steps[0])
    terms = {}
    for number, (at, side, first) in enumerate(steps):
        query, grad, key_all, score, dprob = following
        if number + 1 < len(steps):
            following = operands(*steps[number + 1])
        prob, dscore = weights(at, side, first, score, dprob)
        new = (dot_nn(dscore, query), dot_nn(prob, grad))
        terms[side] = new if first == 0 else tuple(a + b for a, b in zip(terms[side], new))
        query_term = (dot_tn(key_all, dscore) * SCALE).T.astype(jnp.bfloat16)
        dq_side = dq_own if side == 0 else dq_other
        for k in range(2):
            columns = slice(
                (at * heads + first + k) * HEAD_SIZE, (at * heads + first + k + 1) * HEAD_SIZE
            )
            dq_side[:, columns] = query_term[k * half : (k + 1) * half]
        if side == 1 and first + 2 == heads:
            for which in range(2):
                scale = SCALE if which == 0 else 1.0
                columns = slice((2 * at + which) * HEAD_SIZE, (2 * at + which + 1) * HEAD_SIZE)
                own, other = (terms[k][which] * scale for k in range(2))
                for k, (mine, theirs) in enumerate(((own, other), (other, own))):
                    cross = theirs[rows : rows + half]
                    here_too = sides[1 - k][0] == 1
                    place = slice(k * half, (k + 1) * half)
                    g_here[place, columns] = mine[:half] + jnp.where(here_too, cross, 0.0)
                    g_past[place, columns] = (
                        mine[half:rows] + jnp.where(here_too, 0.0, cross)
                    ).astype(jnp.bfloat16)
                joint = own[rows + half :] + other[rows + half :]
                g_near[:, columns] = joint[:rows].astype(jnp.bfloat16)
                g_far[:, columns] = joint[rows:]


def attention(queries, q_other, grad_out, o_other, kv_here, kv_near, kv_past, kv_far, chunk):
    half = queries.shape[0]
    rows = 2 * half
    far_rows = kv_far.shape[0]
    both = 2 * HEAD_SIZE
    count = kv_here.shape[1] // both
    per_core = count * CHUNKS
    group_width = queries.shape[1] // (2 * per_core)
    heads = group_width // HEAD_SIZE

    whole = pl.BlockSpec(memory_space=pltpu.VMEM)
    keys_seen = 3 * rows + far_rows
    return pl.pallas_call(
        functools.partial(attention_kernel, chunk),
        name=f"attention_{chunk}",
        in_specs=[pl.BlockSpec(memory_space=pl.ANY)] * 5 + [whole] * 3,
        out_specs=[whole] * 7,
        out_shape=[
            vmem_shape((half, count * group_width), jnp.bfloat16),
            vmem_shape((half, count * group_width), jnp.bfloat16),
            vmem_shape((count * heads, rows), jnp.float32),
            vmem_shape((rows, count * both), jnp.float32),
            vmem_shape((rows, count * both), jnp.bfloat16),
            vmem_shape((rows, count * both), jnp.bfloat16),
            vmem_shape((far_rows, count * both), jnp.float32),
        ],
        scratch_shapes=[
            pltpu.VMEM((count, 2, half, group_width), jnp.bfloat16),
            pltpu.VMEM((count, 2, half, group_width), jnp.bfloat16),
            pltpu.VMEM((rows, count * both), jnp.bfloat16),
            pltpu.SemaphoreType.DMA((count,)),
            pltpu.SemaphoreType.DMA((count, 2, 2)),
        ],
        compiler_params=pltpu.CompilerParams(vmem_limit_bytes=20 * 1024 * 1024),
        cost_estimate=pl.CostEstimate(
            flops=count * heads * rows * keys_seen * HEAD_SIZE * 20,
            transcendentals=count * heads * rows * keys_seen,
            bytes_accessed=count * (6 * half * group_width * 2 + 5 * rows * both * 4),
        ),
    )(
        *in_hbm(queries, q_other, grad_out, o_other, kv_here), *in_vmem(kv_near, kv_past, kv_far)
    )


def arrange_kernel(chunk, keys, values, k_other, v_other, payload):
    half = keys.shape[0]
    core, _ = pair_position()
    count = payload.shape[1] // (2 * HEAD_SIZE)
    for h in range(count):
        source = head_columns(core * (count * CHUNKS) + chunk * count + h)
        for side, (mine, theirs) in enumerate(((keys, k_other), (values, v_other))):
            to = slice((2 * h + side) * HEAD_SIZE, (2 * h + side + 1) * HEAD_SIZE)
            payload[:half, to] = mine[:, source]
            payload[half:, to] = theirs[:, source]


def arrange(keys, values, k_other, v_other, chunk):
    half, kv_width = keys.shape
    whole = pl.BlockSpec(memory_space=pltpu.VMEM)
    return pl.pallas_call(
        functools.partial(arrange_kernel, chunk),
        name=f"arrange_{chunk}",
        grid=(1,),
        in_specs=[pl.BlockSpec(keys.shape, lambda i: (0, 0))] * 2 + [whole] * 2,
        out_specs=whole,
        out_shape=pltpu.HBM((2 * half, kv_width // CHUNKS), keys.dtype),
    )(keys, values, *in_vmem(k_other, v_other))


def own_rows_kernel(keys, values, out):
    per_core = out.shape[1] // 2
    for core in range(2):
        rows = []
        for h in range(core * per_core, (core + 1) * per_core):
            columns = slice(h * HEAD_SIZE, (h + 1) * HEAD_SIZE)
            rows += [keys[0:1, columns], values[0:1, columns]]
        block = jnp.concatenate([row.astype(jnp.float32) for row in rows], axis=0)
        for peer in range(core, out.shape[0], 2):
            out[peer] = block.astype(out.dtype)


def own_rows(keys, values, peers):
    kv_width = keys.shape[1]
    head = pl.BlockSpec((16, kv_width), lambda i: (0, 0))
    shape = (peers, kv_width // HEAD_SIZE, HEAD_SIZE)
    return pl.pallas_call(
        own_rows_kernel,
        name="own_rows",
        grid=(1,),
        in_specs=[head, head],
        out_specs=pl.BlockSpec(shape, lambda i: (0, 0, 0)),
        out_shape=jax.ShapeDtypeStruct(shape, keys.dtype),
    )(keys, values)


def collect_kernel(chunk, here, near, past, strided, mine, theirs):
    half, width = mine.shape
    core, _ = pair_position()
    extra = jnp.sum(strided[:, :, chunk * width : (chunk + 1) * width], axis=0)
    extra = jnp.where(core == 0, extra, jnp.concatenate([extra[1:2], extra[0:1]], axis=0))
    total = here[...] + near[...].astype(jnp.float32) + past[...].astype(jnp.float32)
    row = lax.broadcasted_iota(jnp.int32, (half, 1), 0)
    mine[...] = (total[:half] + jnp.where(row == 0, extra[0:1], 0.0)).astype(mine.dtype)
    theirs[...] = (total[half:] + jnp.where(row == 0, extra[1:2], 0.0)).astype(theirs.dtype)


def collect(here, near, past, strided, chunk):
    rows, width = here.shape
    half = vmem_shape((rows // 2, width), jnp.bfloat16)
    whole = pl.BlockSpec(memory_space=pltpu.VMEM)
    return pl.pallas_call(
        functools.partial(collect_kernel, chunk),
        name=f"collect_{chunk}",
        in_specs=[whole] * 4,
        out_specs=[whole, whole],
        out_shape=[half, half],
        cost_estimate=pl.CostEstimate(
            flops=rows * width * 4, transcendentals=0, bytes_accessed=rows * width * 10
        ),
    )(*in_vmem(here, near, past, strided))


def place_kernel(*refs):
    here, _ = pair_position()
    *parts, grad_keys, grad_values = refs
    count = parts[0].shape[1] // (2 * HEAD_SIZE)
    for chunk in range(CHUNKS):
        mine, theirs = parts[2 * chunk : 2 * chunk + 2]
        for h in range(count):
            at = chunk * count + h
            for core, block in ((here, mine), (1 - here, theirs)):
                to = head_columns(core * (count * CHUNKS) + at)
                grad_keys[:, to] = block[:, 2 * h * HEAD_SIZE : (2 * h + 1) * HEAD_SIZE]
                grad_values[:, to] = block[:, (2 * h + 1) * HEAD_SIZE : (2 * h + 2) * HEAD_SIZE]


def placed_grads(parts, half, kv_width):
    whole = pl.BlockSpec(memory_space=pltpu.VMEM)
    out = jax.ShapeDtypeStruct((half, kv_width), jnp.bfloat16)
    return pl.pallas_call(
        place_kernel,
        name="place",
        in_specs=[whole] * len(parts),
        out_specs=[whole, whole],
        out_shape=[out, out],
    )(*in_vmem(*parts))


def local(queries, keys, values, grad_out):
    half, kv_width = keys.shape
    kv_heads = kv_width // HEAD_SIZE
    rows = 2 * half
    peers = lax.axis_size("ctx")
    pairs = peers // 2
    assert half == STRIDE and W == 2 * rows and peers % 2 == 0 and kv_heads % (2 * CHUNKS) == 0
    core, _ = pair_position()

    def swap(x):
        return lax.ppermute(x, "ctx", [(i, i ^ 1) for i in range(peers)])

    def shifted(x, by, wrap=True):
        pairs_sent = [(i, (i + by) % peers) for i in range(peers)]
        return lax.ppermute(x, "ctx", [(i, j) for i, j in pairs_sent if wrap or j == i + by])

    def exchanged(x):
        groups = [list(range(parity, peers, 2)) for parity in range(2)]
        return lax.all_to_all(x, "ctx", 0, 0, axis_index_groups=groups)

    def joined(mine, theirs):
        return jnp.where(
            core == 0,
            jnp.concatenate([mine, theirs], axis=1),
            jnp.concatenate([theirs, mine], axis=1),
        )

    sent = own_rows(keys, values, peers)
    k_other, v_other, sent = lax.optimization_barrier((swap(keys), swap(values), sent))
    far = lax.all_to_all(sent, "ctx", 0, 0, tiled=True)
    here = [arrange(keys, values, k_other, v_other, chunk) for chunk in range(CHUNKS)]
    near, past = [], []
    for chunk in range(CHUNKS):
        payload = here[chunk]
        if chunk > 0:
            payload, _ = lax.optimization_barrier((payload, far))
        near.append(shifted(payload, 2))
        past.append(shifted(payload, 4))
    q_sent, o_sent, _ = lax.optimization_barrier((queries, grad_out, here[0]))
    q_other, o_other = swap(q_sent), swap(o_sent)

    dq_own, dq_other, norms, sums, far_terms = [], [], [], [], []
    for chunk in range(CHUNKS):
        out = attention(
            queries,
            q_other,
            grad_out,
            o_other,
            here[chunk],
            near[chunk],
            past[chunk],
            far,
            chunk,
        )
        last = chunk == CHUNKS - 1
        sums.append((out[3], shifted(out[4], -2, last), shifted(out[5], -4, last)))
        dq_own.append(out[0])
        dq_other.append(swap(out[1]))
        norms.append(out[2])
        far, _ = lax.optimization_barrier((far, out[2]))
        far_terms.append(out[6])

    terms, *_ = lax.optimization_barrier((jnp.concatenate(far_terms, axis=1), *sums[0][1:]))
    strided_terms = exchanged(terms.reshape(pairs, 2, kv_width))
    grad_queries = joined(jnp.concatenate(dq_own, axis=1), jnp.concatenate(dq_other, axis=1))
    norm = jnp.concatenate(norms, axis=0)
    norm_sent, *_ = lax.optimization_barrier((norm[:, half:], *sums[0][1:]))
    log_norm = joined(norm[:, :half].T, swap(norm_sent).T)
    parts = []
    for chunk, (own, near_terms, past_terms) in enumerate(sums):
        if chunk > 0:
            own, grad_queries, log_norm, _ = lax.optimization_barrier(
                (own, grad_queries, log_norm, parts[-2])
            )
        mine, theirs = collect(own, near_terms, past_terms, strided_terms, chunk)
        parts += [mine, swap(theirs)]
    grad_keys, grad_values = placed_grads(parts, half, kv_width)
    return (grad_queries, grad_keys, grad_values, log_norm)


def solution(mesh):
    placed = P(("groups", "ctx"), "head")
    return jax.shard_map(
        local,
        mesh=mesh,
        in_specs=(placed,) * 4,
        out_specs=(placed,) * 4,
        check_vma=False,
    )
```

```python
import functools
import math

import jax
import jax.numpy as jnp
from jax import lax
from jax.experimental import pallas as pl
from jax.experimental.pallas import tpu as pltpu
from jax.sharding import PartitionSpec as P

HEAD_SIZE = 128
W = 512
STRIDE = 128
CHUNKS = 2

NEG_FILL = -1e30
SCALE = 1.0 / math.sqrt(HEAD_SIZE)


def vmem_shape(shape, dtype):
    return pltpu.VMEM(shape, dtype)


def in_hbm(*arrays):
    return [pltpu.with_memory_space_constraint(x, pltpu.HBM) for x in arrays]


def in_vmem(*arrays):
    return [pltpu.with_memory_space_constraint(x, pltpu.VMEM) for x in arrays]


def head_columns(which, width=HEAD_SIZE):
    return pl.ds(pl.multiple_of(which * width, width), width)


def pair_position():
    index = lax.axis_index("ctx")
    return index & 1, index >> 1


def dot_nt(left, right):
    return lax.dot_general(
        left, right, (((1,), (1,)), ((), ())), preferred_element_type=jnp.float32
    )


def dot_nn(left, right):
    return lax.dot_general(
        left, right, (((1,), (0,)), ((), ())), preferred_element_type=jnp.float32
    )


def dot_tn(left, right):
    return lax.dot_general(
        left, right, (((0,), (0,)), ((), ())), preferred_element_type=jnp.float32
    )


def attend(
    chunk,
    staged_q,
    staged_o,
    here,
    kv_near,
    kv_past,
    kv_far,
    dq_own,
    dq_other,
    norm,
    g_here,
    g_near,
    g_past,
    g_far,
):
    half = staged_q.shape[1]
    rows = 2 * half
    far_rows = kv_far.shape[0]
    both = 2 * HEAD_SIZE
    count = kv_near.shape[1] // both
    width = dq_own.shape[1]
    heads = width // (count * HEAD_SIZE)
    core, pair = pair_position()
    wide = (half, rows)
    lane = lax.broadcasted_iota(jnp.int32, wide, 1) % half
    lower = lax.broadcasted_iota(jnp.int32, wide, 0) <= lane
    far_at = lax.broadcasted_iota(jnp.int32, (far_rows, rows), 0)
    far_lane = lax.broadcasted_iota(jnp.int32, (far_rows, rows), 1) % half
    far_token = far_at * half
    near_bias = jnp.where(pair >= 1, 0.0, NEG_FILL)
    past_bias = jnp.where(pair >= 2, 0.0, NEG_FILL)
    sides = []
    for side in range(2):
        later = core if side == 0 else 1 - core
        sides.append(
            (
                later,
                far_token <= pair * rows + later * half + far_lane - W,
                jnp.where(later == 0, past_bias, 0.0),
            )
        )

    def keys_of(at, side, which):
        columns = slice((2 * at + which) * HEAD_SIZE, (2 * at + which + 1) * HEAD_SIZE)
        far_row = 2 * (chunk * count + at) + which
        same = slice(side * half, (side + 1) * half)
        cross = slice((1 - side) * half, (2 - side) * half)
        full = jnp.where(sides[side][0] == 1, here[cross, columns], kv_past[cross, columns])
        return jnp.concatenate(
            [
                here[same, columns],
                kv_past[same, columns],
                full,
                kv_near[:, columns],
                kv_far[:, far_row, :],
            ],
            axis=0,
        )

    def operands(at, side, first):
        query, grad = (
            jnp.concatenate(
                [
                    staged[side, :, head * HEAD_SIZE : (head + 1) * HEAD_SIZE]
                    for head in (at * heads + first, at * heads + first + 1)
                ],
                axis=0,
            )
            for staged in (staged_q, staged_o)
        )
        key_all, value_all = keys_of(at, side, 0), keys_of(at, side, 1)
        return query, grad, key_all, dot_nt(key_all, query), dot_nt(value_all, grad)

    def merged(whole, bias):
        edge = jnp.where(lower, whole[:half], whole[half:rows] + bias)
        return edge, whole[rows : rows + half], whole[rows + half : 2 * rows + half]

    def reduced(op, parts):
        out = [op(part, axis=0, keepdims=True) for part in parts]
        return out

    def weights(at, side, first, score, dprob):
        _, far_open, full_bias = sides[side]
        edge, full, near = merged(score, past_bias)
        parts = [
            edge,
            full + full_bias,
            near + near_bias,
            jnp.where(far_open, score[2 * rows + half :], NEG_FILL),
        ]
        top = functools.reduce(jnp.maximum, reduced(jnp.max, parts))
        parts = [jnp.exp2((part - top) * (SCALE * math.log2(math.e))) for part in parts]
        total = sum(reduced(jnp.sum, parts))
        log_total = top * SCALE + jnp.log(total)
        for k in range(2):
            row = at * heads + first + k
            norm[row : row + 1, side * half : (side + 1) * half] = log_total[
                :, k * half : (k + 1) * half
            ]
        inverse = 1.0 / total
        parts = [part * inverse for part in parts]
        d_parts = [*merged(dprob, 0.0), dprob[2 * rows + half :]]
        delta = sum(reduced(jnp.sum, [part * d_part for part, d_part in zip(parts, d_parts)]))
        d_parts = [part * (d_part - delta) for part, d_part in zip(parts, d_parts)]

        def split(edge, *others):
            return jnp.concatenate(
                [
                    jnp.where(lower, edge, 0.0).astype(jnp.bfloat16),
                    jnp.where(lower, 0.0, edge).astype(jnp.bfloat16),
                    *(part.astype(jnp.bfloat16) for part in others),
                ],
                axis=0,
            )

        return split(*parts), split(*d_parts)

    steps = [
        (at, side, first)
        for at in range(count)
        for side in range(2)
        for first in range(0, heads, 2)
    ]
    following = operands(*steps[0])
    terms = {}
    for number, (at, side, first) in enumerate(steps):
        query, grad, key_all, score, dprob = following
        if number + 1 < len(steps):
            following = operands(*steps[number + 1])
        prob, dscore = weights(at, side, first, score, dprob)
        new = (dot_nn(dscore, query), dot_nn(prob, grad))
        terms[side] = new if first == 0 else tuple(a + b for a, b in zip(terms[side], new))
        query_term = (dot_tn(key_all, dscore) * SCALE).T.astype(jnp.bfloat16)
        dq_side = dq_own if side == 0 else dq_other
        for k in range(2):
            columns = slice(
                (at * heads + first + k) * HEAD_SIZE, (at * heads + first + k + 1) * HEAD_SIZE
            )
            dq_side[:, columns] = query_term[k * half : (k + 1) * half]
        if side == 1 and first + 2 == heads:
            for which in range(2):
                scale = SCALE if which == 0 else 1.0
                columns = slice((2 * at + which) * HEAD_SIZE, (2 * at + which + 1) * HEAD_SIZE)
                own, other = (terms[k][which] * scale for k in range(2))
                for k, (mine, theirs) in enumerate(((own, other), (other, own))):
                    cross = theirs[rows : rows + half]
                    here_too = sides[1 - k][0] == 1
                    place = slice(k * half, (k + 1) * half)
                    g_here[place, columns] = mine[:half] + jnp.where(here_too, cross, 0.0)
                    g_past[place, columns] = (
                        mine[half:rows] + jnp.where(here_too, 0.0, cross)
                    ).astype(jnp.bfloat16)
                joint = own[rows + half :] + other[rows + half :]
                g_near[:, columns] = joint[:rows].astype(jnp.bfloat16)
                g_far[:, columns] = joint[rows:]


def stage_copies(chunk, sources, targets, done):
    q_own, q_other, o_own, o_other = sources[:4]
    staged_q, staged_o, here = targets
    core, _ = pair_position()
    columns = head_columns(core * CHUNKS + chunk, staged_q.shape[2])
    pieces = [
        (sources[4 + chunk], here),
        (q_own.at[:, columns], staged_q.at[0]),
        (o_own.at[:, columns], staged_o.at[0]),
        (q_other.at[:, columns], staged_q.at[1]),
        (o_other.at[:, columns], staged_o.at[1]),
    ]
    return [
        pltpu.make_async_copy(source, target, done.at[chunk, number])
        for number, (source, target) in enumerate(pieces)
    ]


def first_kernel(*refs):
    sources, blocks, outs = refs[: 4 + CHUNKS], refs[4 + CHUNKS : 7 + CHUNKS], refs[7 + CHUNKS :]
    mine, *later = (
        stage_copies(chunk, sources, targets, outs[-1])
        for chunk, targets in enumerate(
            [outs[-4:-1]] + [outs[7 + 3 * k : 10 + 3 * k] for k in range(CHUNKS - 1)]
        )
    )
    for copy in mine + sum(later, []):
        copy.start()
    for copy in mine:
        copy.wait()
    attend(0, *outs[-4:-1], *blocks, *outs[:7])
    for copy in sum(later, []):
        copy.wait()


def attention(chunk, operands, kv_near, kv_past, kv_far, width):
    half = kv_near.shape[0] // 2
    rows = 2 * half
    far_rows = kv_far.shape[0]
    both = 2 * HEAD_SIZE
    count = kv_near.shape[1] // both
    heads = width // (count * HEAD_SIZE)
    whole = pl.BlockSpec(memory_space=pltpu.VMEM)
    keys_seen = 3 * rows + far_rows
    staged = [(2, half, width), (2, half, width), (rows, count * both)]
    outs = [
        vmem_shape((half, width), jnp.bfloat16),
        vmem_shape((half, width), jnp.bfloat16),
        vmem_shape((count * heads, rows), jnp.float32),
        vmem_shape((rows, count * both), jnp.float32),
        vmem_shape((rows, count * both), jnp.bfloat16),
        vmem_shape((rows, count * both), jnp.bfloat16),
        vmem_shape((far_rows, count * both), jnp.float32),
    ]
    if chunk == 0:
        outs += [vmem_shape(shape, jnp.bfloat16) for shape in staged] * (CHUNKS - 1)
        operands = in_hbm(*operands)
        scratch = [pltpu.VMEM(shape, jnp.bfloat16) for shape in staged]
        scratch.append(pltpu.SemaphoreType.DMA((CHUNKS, 5)))
    else:
        operands = in_vmem(*operands)
        scratch = []
    space = pl.BlockSpec(memory_space=pl.ANY) if chunk == 0 else whole
    return pl.pallas_call(
        first_kernel if chunk == 0 else functools.partial(attend, chunk),
        name=f"attention_{chunk}",
        in_specs=[space] * len(operands) + [whole] * 3,
        out_specs=[whole] * len(outs),
        out_shape=outs,
        scratch_shapes=scratch,
        compiler_params=pltpu.CompilerParams(vmem_limit_bytes=20 * 1024 * 1024),
        cost_estimate=pl.CostEstimate(
            flops=count * heads * rows * keys_seen * HEAD_SIZE * 20,
            transcendentals=count * heads * rows * keys_seen,
            bytes_accessed=6 * half * width * 2 + count * 5 * rows * both * 4,
        ),
    )(*operands, *in_vmem(kv_near, kv_past, kv_far))


def arrange_kernel(chunk, keys, values, k_other, v_other, payload):
    half = keys.shape[0]
    core, _ = pair_position()
    count = payload.shape[1] // (2 * HEAD_SIZE)
    for h in range(count):
        source = head_columns(core * (count * CHUNKS) + chunk * count + h)
        for side, (mine, theirs) in enumerate(((keys, k_other), (values, v_other))):
            to = slice((2 * h + side) * HEAD_SIZE, (2 * h + side + 1) * HEAD_SIZE)
            payload[:half, to] = mine[:, source]
            payload[half:, to] = theirs[:, source]


def arrange(keys, values, k_other, v_other, chunk):
    half, kv_width = keys.shape
    whole = pl.BlockSpec(memory_space=pltpu.VMEM)
    return pl.pallas_call(
        functools.partial(arrange_kernel, chunk),
        name=f"arrange_{chunk}",
        grid=(1,),
        in_specs=[pl.BlockSpec(keys.shape, lambda i: (0, 0))] * 2 + [whole] * 2,
        out_specs=whole,
        out_shape=pltpu.HBM((2 * half, kv_width // CHUNKS), keys.dtype),
    )(keys, values, *in_vmem(k_other, v_other))


def own_rows_kernel(keys, values, out):
    per_core = out.shape[1] // 2
    for core in range(2):
        rows = []
        for h in range(core * per_core, (core + 1) * per_core):
            columns = slice(h * HEAD_SIZE, (h + 1) * HEAD_SIZE)
            rows += [keys[0:1, columns], values[0:1, columns]]
        block = jnp.concatenate([row.astype(jnp.float32) for row in rows], axis=0)
        for peer in range(core, out.shape[0], 2):
            out[peer] = block.astype(out.dtype)


def own_rows(keys, values, peers):
    kv_width = keys.shape[1]
    head = pl.BlockSpec((16, kv_width), lambda i: (0, 0))
    shape = (peers, kv_width // HEAD_SIZE, HEAD_SIZE)
    return pl.pallas_call(
        own_rows_kernel,
        name="own_rows",
        grid=(1,),
        in_specs=[head, head],
        out_specs=pl.BlockSpec(shape, lambda i: (0, 0, 0)),
        out_shape=jax.ShapeDtypeStruct(shape, keys.dtype),
    )(keys, values)


def collect_kernel(chunk, here, near, past, strided, mine, theirs):
    half, width = mine.shape
    core, _ = pair_position()
    extra = jnp.sum(strided[:, :, chunk * width : (chunk + 1) * width], axis=0)
    extra = jnp.where(core == 0, extra, jnp.concatenate([extra[1:2], extra[0:1]], axis=0))
    total = here[...] + near[...].astype(jnp.float32) + past[...].astype(jnp.float32)
    row = lax.broadcasted_iota(jnp.int32, (half, 1), 0)
    mine[...] = (total[:half] + jnp.where(row == 0, extra[0:1], 0.0)).astype(mine.dtype)
    theirs[...] = (total[half:] + jnp.where(row == 0, extra[1:2], 0.0)).astype(theirs.dtype)


def collect(here, near, past, strided, chunk):
    rows, width = here.shape
    half = vmem_shape((rows // 2, width), jnp.bfloat16)
    whole = pl.BlockSpec(memory_space=pltpu.VMEM)
    return pl.pallas_call(
        functools.partial(collect_kernel, chunk),
        name=f"collect_{chunk}",
        in_specs=[whole] * 4,
        out_specs=[whole, whole],
        out_shape=[half, half],
        cost_estimate=pl.CostEstimate(
            flops=rows * width * 4, transcendentals=0, bytes_accessed=rows * width * 10
        ),
    )(*in_vmem(here, near, past, strided))


def place_kernel(*refs):
    here, _ = pair_position()
    *parts, grad_keys, grad_values = refs
    count = parts[0].shape[1] // (2 * HEAD_SIZE)
    for chunk in range(CHUNKS):
        mine, theirs = parts[2 * chunk : 2 * chunk + 2]
        for h in range(count):
            at = chunk * count + h
            for core, block in ((here, mine), (1 - here, theirs)):
                to = head_columns(core * (count * CHUNKS) + at)
                grad_keys[:, to] = block[:, 2 * h * HEAD_SIZE : (2 * h + 1) * HEAD_SIZE]
                grad_values[:, to] = block[:, (2 * h + 1) * HEAD_SIZE : (2 * h + 2) * HEAD_SIZE]


def placed_grads(parts, half, kv_width):
    whole = pl.BlockSpec(memory_space=pltpu.VMEM)
    out = jax.ShapeDtypeStruct((half, kv_width), jnp.bfloat16)
    return pl.pallas_call(
        place_kernel,
        name="place",
        in_specs=[whole] * len(parts),
        out_specs=[whole, whole],
        out_shape=[out, out],
    )(*in_vmem(*parts))


def local(queries, keys, values, grad_out):
    half, kv_width = keys.shape
    kv_heads = kv_width // HEAD_SIZE
    rows = 2 * half
    peers = lax.axis_size("ctx")
    pairs = peers // 2
    assert half == STRIDE and W == 2 * rows and peers % 2 == 0 and kv_heads % (2 * CHUNKS) == 0
    core, _ = pair_position()

    def swap(x):
        return lax.ppermute(x, "ctx", [(i, i ^ 1) for i in range(peers)])

    def shifted(x, by, wrap=True):
        pairs_sent = [(i, (i + by) % peers) for i in range(peers)]
        return lax.ppermute(x, "ctx", [(i, j) for i, j in pairs_sent if wrap or j == i + by])

    def exchanged(x):
        groups = [list(range(parity, peers, 2)) for parity in range(2)]
        return lax.all_to_all(x, "ctx", 0, 0, axis_index_groups=groups)

    def joined(mine, theirs):
        return jnp.where(
            core == 0,
            jnp.concatenate([mine, theirs], axis=1),
            jnp.concatenate([theirs, mine], axis=1),
        )

    sent = own_rows(keys, values, peers)
    k_other, v_other, sent = lax.optimization_barrier((swap(keys), swap(values), sent))
    far = lax.all_to_all(sent, "ctx", 0, 0, tiled=True)
    here = [arrange(keys, values, k_other, v_other, chunk) for chunk in range(CHUNKS)]
    near, past = [], []
    for chunk in range(CHUNKS):
        payload = here[chunk]
        if chunk > 0:
            payload, _ = lax.optimization_barrier((payload, far))
        near.append(shifted(payload, 2))
        past.append(shifted(payload, 4))
    q_sent, o_sent, _ = lax.optimization_barrier((queries, grad_out, here[0]))
    q_other, o_other = swap(q_sent), swap(o_sent)

    width = queries.shape[1] // (2 * CHUNKS)
    operands = (queries, q_other, grad_out, o_other, *here)
    dq_own, dq_other, norms, sums, far_terms = [], [], [], [], []
    for chunk in range(CHUNKS):
        out = attention(chunk, operands, near[chunk], past[chunk], far, width)
        if chunk == 0:
            staged = out[7:]
        operands = staged[3 * chunk : 3 * chunk + 3]
        last = chunk == CHUNKS - 1
        sums.append((out[3], shifted(out[4], -2, last), shifted(out[5], -4, last)))
        dq_own.append(out[0])
        dq_other.append(swap(out[1]))
        norms.append(out[2])
        far, _ = lax.optimization_barrier((far, out[2]))
        far_terms.append(out[6])

    terms, *_ = lax.optimization_barrier((jnp.concatenate(far_terms, axis=1), *sums[0][1:]))
    strided_terms = exchanged(terms.reshape(pairs, 2, kv_width))
    grad_queries = joined(jnp.concatenate(dq_own, axis=1), jnp.concatenate(dq_other, axis=1))
    norm = jnp.concatenate(norms, axis=0)
    norm_sent, *_ = lax.optimization_barrier((norm[:, half:], *sums[0][1:]))
    log_norm = joined(norm[:, :half].T, swap(norm_sent).T)
    parts = []
    for chunk, (own, near_terms, past_terms) in enumerate(sums):
        if chunk > 0:
            own, grad_queries, log_norm, _ = lax.optimization_barrier(
                (own, grad_queries, log_norm, parts[-2])
            )
        mine, theirs = collect(own, near_terms, past_terms, strided_terms, chunk)
        parts += [mine, swap(theirs)]
    grad_keys, grad_values = placed_grads(parts, half, kv_width)
    return (grad_queries, grad_keys, grad_values, log_norm)


def solution(mesh):
    placed = P(("groups", "ctx"), "head")
    return jax.shard_map(
        local,
        mesh=mesh,
        in_specs=(placed,) * 4,
        out_specs=(placed,) * 4,
        check_vma=False,
    )
```

```python
import functools
import math

import jax
import jax.numpy as jnp
from jax import lax
from jax.experimental import pallas as pl
from jax.experimental.pallas import tpu as pltpu
from jax.sharding import PartitionSpec as P

HEAD_SIZE = 128
W = 512
STRIDE = 128
CHUNKS = 2

NEG_FILL = -1e30
SCALE = 1.0 / math.sqrt(HEAD_SIZE)


def vmem_shape(shape, dtype):
    return pltpu.VMEM(shape, dtype)


def in_hbm(*arrays):
    return [pltpu.with_memory_space_constraint(x, pltpu.HBM) for x in arrays]


def in_vmem(*arrays):
    return [pltpu.with_memory_space_constraint(x, pltpu.VMEM) for x in arrays]


def head_columns(which, width=HEAD_SIZE):
    return pl.ds(pl.multiple_of(which * width, width), width)


def pair_position():
    index = lax.axis_index("ctx")
    return index & 1, index >> 1


def dot_nt(left, right):
    return lax.dot_general(
        left, right, (((1,), (1,)), ((), ())), preferred_element_type=jnp.float32
    )


def dot_nn(left, right):
    return lax.dot_general(
        left, right, (((1,), (0,)), ((), ())), preferred_element_type=jnp.float32
    )


def dot_tn(left, right):
    return lax.dot_general(
        left, right, (((0,), (0,)), ((), ())), preferred_element_type=jnp.float32
    )


def attend(
    chunk,
    staged_q,
    staged_o,
    here,
    kv_near,
    kv_past,
    kv_far,
    dq_own,
    dq_other,
    norm,
    g_here,
    g_near,
    g_past,
    g_far,
):
    half = staged_q.shape[1]
    rows = 2 * half
    far_rows = kv_far.shape[0]
    both = 2 * HEAD_SIZE
    count = kv_near.shape[1] // both
    width = dq_own.shape[1]
    heads = width // (count * HEAD_SIZE)
    core, pair = pair_position()
    wide = (half, rows)
    lane = lax.broadcasted_iota(jnp.int32, wide, 1) % half
    lower = lax.broadcasted_iota(jnp.int32, wide, 0) <= lane
    far_at = lax.broadcasted_iota(jnp.int32, (far_rows, rows), 0)
    far_lane = lax.broadcasted_iota(jnp.int32, (far_rows, rows), 1) % half
    far_token = far_at * half
    near_bias = jnp.where(pair >= 1, 0.0, NEG_FILL)
    past_bias = jnp.where(pair >= 2, 0.0, NEG_FILL)
    sides = []
    for side in range(2):
        later = core if side == 0 else 1 - core
        sides.append(
            (
                later,
                far_token <= pair * rows + later * half + far_lane - W,
                jnp.where(later == 0, past_bias, 0.0),
            )
        )

    def keys_of(at, side, which):
        columns = slice((2 * at + which) * HEAD_SIZE, (2 * at + which + 1) * HEAD_SIZE)
        far_row = 2 * (chunk * count + at) + which
        same = slice(side * half, (side + 1) * half)
        cross = slice((1 - side) * half, (2 - side) * half)
        full = jnp.where(sides[side][0] == 1, here[cross, columns], kv_past[cross, columns])
        return jnp.concatenate(
            [
                here[same, columns],
                kv_past[same, columns],
                full,
                kv_near[:, columns],
                kv_far[:, far_row, :],
            ],
            axis=0,
        )

    def operands(at, side, first):
        query, grad = (
            jnp.concatenate(
                [
                    staged[side, :, head * HEAD_SIZE : (head + 1) * HEAD_SIZE]
                    for head in (at * heads + first, at * heads + first + 1)
                ],
                axis=0,
            )
            for staged in (staged_q, staged_o)
        )
        key_all, value_all = keys_of(at, side, 0), keys_of(at, side, 1)
        return query, grad, key_all, dot_nt(key_all, query), dot_nt(value_all, grad)

    def merged(whole, bias):
        edge = jnp.where(lower, whole[:half], whole[half:rows] + bias)
        return edge, whole[rows : rows + half], whole[rows + half : 2 * rows + half]

    def reduced(op, parts):
        out = [op(part, axis=0, keepdims=True) for part in parts]
        return out

    def weights(at, side, first, score, dprob):
        _, far_open, full_bias = sides[side]
        edge, full, near = merged(score, past_bias)
        parts = [
            edge,
            full + full_bias,
            near + near_bias,
            jnp.where(far_open, score[2 * rows + half :], NEG_FILL),
        ]
        top = functools.reduce(jnp.maximum, reduced(jnp.max, parts))
        parts = [jnp.exp2((part - top) * (SCALE * math.log2(math.e))) for part in parts]
        total = sum(reduced(jnp.sum, parts))
        log_total = top * SCALE + jnp.log(total)
        for k in range(2):
            row = at * heads + first + k
            norm[row : row + 1, side * half : (side + 1) * half] = log_total[
                :, k * half : (k + 1) * half
            ]
        inverse = 1.0 / total
        parts = [part * inverse for part in parts]
        d_parts = [*merged(dprob, 0.0), dprob[2 * rows + half :]]
        delta = sum(reduced(jnp.sum, [part * d_part for part, d_part in zip(parts, d_parts)]))
        d_parts = [part * (d_part - delta) for part, d_part in zip(parts, d_parts)]

        def split(edge, *others):
            return jnp.concatenate(
                [
                    jnp.where(lower, edge, 0.0).astype(jnp.bfloat16),
                    jnp.where(lower, 0.0, edge).astype(jnp.bfloat16),
                    *(part.astype(jnp.bfloat16) for part in others),
                ],
                axis=0,
            )

        return split(*parts), split(*d_parts)

    steps = [
        (at, side, first)
        for at in range(count)
        for side in range(2)
        for first in range(0, heads, 2)
    ]
    following = operands(*steps[0])
    terms = {}
    for number, (at, side, first) in enumerate(steps):
        query, grad, key_all, score, dprob = following
        if number + 1 < len(steps):
            following = operands(*steps[number + 1])
        prob, dscore = weights(at, side, first, score, dprob)
        new = (dot_nn(dscore, query), dot_nn(prob, grad))
        terms[side] = new if first == 0 else tuple(a + b for a, b in zip(terms[side], new))
        query_term = (dot_tn(key_all, dscore) * SCALE).T.astype(jnp.bfloat16)
        dq_side = dq_own if side == 0 else dq_other
        for k in range(2):
            columns = slice(
                (at * heads + first + k) * HEAD_SIZE, (at * heads + first + k + 1) * HEAD_SIZE
            )
            dq_side[:, columns] = query_term[k * half : (k + 1) * half]
        if side == 1 and first + 2 == heads:
            for which in range(2):
                scale = SCALE if which == 0 else 1.0
                columns = slice((2 * at + which) * HEAD_SIZE, (2 * at + which + 1) * HEAD_SIZE)
                own, other = (terms[k][which] * scale for k in range(2))
                for k, (mine, theirs) in enumerate(((own, other), (other, own))):
                    cross = theirs[rows : rows + half]
                    here_too = sides[1 - k][0] == 1
                    place = slice(k * half, (k + 1) * half)
                    g_here[place, columns] = mine[:half] + jnp.where(here_too, cross, 0.0)
                    g_past[place, columns] = (
                        mine[half:rows] + jnp.where(here_too, 0.0, cross)
                    ).astype(jnp.bfloat16)
                joint = own[rows + half :] + other[rows + half :]
                g_near[:, columns] = joint[:rows].astype(jnp.bfloat16)
                g_far[:, 2 * (chunk * count + at) + which, :] = joint[rows:]


def stage_copies(chunk, sources, targets, done):
    q_own, q_other, o_own, o_other = sources[:4]
    staged_q, staged_o, here = targets
    core, _ = pair_position()
    columns = head_columns(core * CHUNKS + chunk, staged_q.shape[2])
    pieces = [
        (sources[4 + chunk], here),
        (q_own.at[:, columns], staged_q.at[0]),
        (o_own.at[:, columns], staged_o.at[0]),
        (q_other.at[:, columns], staged_q.at[1]),
        (o_other.at[:, columns], staged_o.at[1]),
    ]
    return [
        pltpu.make_async_copy(source, target, done.at[chunk, number])
        for number, (source, target) in enumerate(pieces)
    ]


def first_kernel(*refs):
    sources, blocks, outs = refs[: 4 + CHUNKS], refs[4 + CHUNKS : 7 + CHUNKS], refs[7 + CHUNKS :]
    mine, *later = (
        stage_copies(chunk, sources, targets, outs[-1])
        for chunk, targets in enumerate(
            [outs[-4:-1]] + [outs[7 + 3 * k : 10 + 3 * k] for k in range(CHUNKS - 1)]
        )
    )
    for copy in mine + sum(later, []):
        copy.start()
    for copy in mine:
        copy.wait()
    attend(0, *outs[-4:-1], *blocks, *outs[:7])
    for copy in sum(later, []):
        copy.wait()


def later_kernel(chunk, *refs):
    before, g_far = refs[6], refs[-1]
    g_far[:, : before.shape[1], :] = before[...]
    attend(chunk, *refs[:6], *refs[7:])


def attention(chunk, operands, kv_near, kv_past, kv_far, far_terms, width):
    half = kv_near.shape[0] // 2
    rows = 2 * half
    far_rows = kv_far.shape[0]
    both = 2 * HEAD_SIZE
    count = kv_near.shape[1] // both
    heads = width // (count * HEAD_SIZE)
    whole = pl.BlockSpec(memory_space=pltpu.VMEM)
    keys_seen = 3 * rows + far_rows
    staged = [(2, half, width), (2, half, width), (rows, count * both)]
    outs = [
        vmem_shape((half, width), jnp.bfloat16),
        vmem_shape((half, width), jnp.bfloat16),
        vmem_shape((count * heads, rows), jnp.float32),
        vmem_shape((rows, count * both), jnp.float32),
        vmem_shape((rows, count * both), jnp.bfloat16),
        vmem_shape((rows, count * both), jnp.bfloat16),
        vmem_shape((far_rows, 2 * count * (chunk + 1), HEAD_SIZE), jnp.float32),
    ]
    blocks = [kv_near, kv_past, kv_far]
    if chunk == 0:
        outs += [vmem_shape(shape, jnp.bfloat16) for shape in staged] * (CHUNKS - 1)
        operands = in_hbm(*operands)
        scratch = [pltpu.VMEM(shape, jnp.bfloat16) for shape in staged]
        scratch.append(pltpu.SemaphoreType.DMA((CHUNKS, 5)))
    else:
        operands = in_vmem(*operands)
        blocks.append(far_terms)
        scratch = []
    space = pl.BlockSpec(memory_space=pl.ANY) if chunk == 0 else whole
    return pl.pallas_call(
        first_kernel if chunk == 0 else functools.partial(later_kernel, chunk),
        name=f"attention_{chunk}",
        in_specs=[space] * len(operands) + [whole] * len(blocks),
        out_specs=[whole] * len(outs),
        out_shape=outs,
        scratch_shapes=scratch,
        compiler_params=pltpu.CompilerParams(vmem_limit_bytes=20 * 1024 * 1024),
        cost_estimate=pl.CostEstimate(
            flops=count * heads * rows * keys_seen * HEAD_SIZE * 20,
            transcendentals=count * heads * rows * keys_seen,
            bytes_accessed=6 * half * width * 2 + count * 5 * rows * both * 4,
        ),
    )(*operands, *in_vmem(*blocks))


def arrange_kernel(chunk, keys, values, k_other, v_other, payload):
    half = keys.shape[0]
    core, _ = pair_position()
    count = payload.shape[1] // (2 * HEAD_SIZE)
    for h in range(count):
        source = head_columns(core * (count * CHUNKS) + chunk * count + h)
        for side, (mine, theirs) in enumerate(((keys, k_other), (values, v_other))):
            to = slice((2 * h + side) * HEAD_SIZE, (2 * h + side + 1) * HEAD_SIZE)
            payload[:half, to] = mine[:, source]
            payload[half:, to] = theirs[:, source]


def arrange(keys, values, k_other, v_other, chunk):
    half, kv_width = keys.shape
    whole = pl.BlockSpec(memory_space=pltpu.VMEM)
    return pl.pallas_call(
        functools.partial(arrange_kernel, chunk),
        name=f"arrange_{chunk}",
        grid=(1,),
        in_specs=[pl.BlockSpec(keys.shape, lambda i: (0, 0))] * 2 + [whole] * 2,
        out_specs=whole,
        out_shape=pltpu.HBM((2 * half, kv_width // CHUNKS), keys.dtype),
    )(keys, values, *in_vmem(k_other, v_other))


def own_rows_kernel(keys, values, out):
    per_core = out.shape[1] // 2
    for core in range(2):
        rows = []
        for h in range(core * per_core, (core + 1) * per_core):
            columns = slice(h * HEAD_SIZE, (h + 1) * HEAD_SIZE)
            rows += [keys[0:1, columns], values[0:1, columns]]
        block = jnp.concatenate([row.astype(jnp.float32) for row in rows], axis=0)
        for peer in range(core, out.shape[0], 2):
            out[peer] = block.astype(out.dtype)


def own_rows(keys, values, peers):
    kv_width = keys.shape[1]
    head = pl.BlockSpec((16, kv_width), lambda i: (0, 0))
    shape = (peers, kv_width // HEAD_SIZE, HEAD_SIZE)
    return pl.pallas_call(
        own_rows_kernel,
        name="own_rows",
        grid=(1,),
        in_specs=[head, head],
        out_specs=pl.BlockSpec(shape, lambda i: (0, 0, 0)),
        out_shape=jax.ShapeDtypeStruct(shape, keys.dtype),
    )(keys, values)


def collect_kernel(*refs):
    *terms, strided, mine, theirs = refs
    half = mine.shape[0]
    width = terms[0].shape[1]
    core, _ = pair_position()
    own, other = (
        jnp.concatenate(
            [
                jnp.sum(strided[:, k, column, :], axis=0, keepdims=True)
                for column in range(strided.shape[2])
            ],
            axis=1,
        )
        for k in range(2)
    )
    extra = jnp.where(
        core == 0, jnp.concatenate([own, other], axis=0), jnp.concatenate([other, own], axis=0)
    )
    row = lax.broadcasted_iota(jnp.int32, (half, 1), 0)
    for chunk in range(CHUNKS):
        here, near, past = terms[3 * chunk : 3 * chunk + 3]
        columns = slice(chunk * width, (chunk + 1) * width)
        total = here[...] + near[...].astype(jnp.float32) + past[...].astype(jnp.float32)
        for k, out in enumerate((mine, theirs)):
            added = jnp.where(row == 0, extra[k : k + 1, columns], 0.0)
            out[:, columns] = (total[k * half : (k + 1) * half] + added).astype(out.dtype)


def collect(terms, strided):
    rows, width = terms[0].shape
    half = vmem_shape((rows // 2, CHUNKS * width), jnp.bfloat16)
    whole = pl.BlockSpec(memory_space=pltpu.VMEM)
    return pl.pallas_call(
        collect_kernel,
        name="collect",
        in_specs=[whole] * (len(terms) + 1),
        out_specs=[whole, whole],
        out_shape=[half, half],
        cost_estimate=pl.CostEstimate(
            flops=CHUNKS * rows * width * 4,
            transcendentals=0,
            bytes_accessed=CHUNKS * rows * width * 10,
        ),
    )(*in_vmem(*terms, strided))


def place_kernel(mine, theirs, grad_keys, grad_values):
    here, _ = pair_position()
    count = mine.shape[1] // (2 * HEAD_SIZE)
    for h in range(count):
        for core, block in ((here, mine), (1 - here, theirs)):
            to = head_columns(core * count + h)
            grad_keys[:, to] = block[:, 2 * h * HEAD_SIZE : (2 * h + 1) * HEAD_SIZE]
            grad_values[:, to] = block[:, (2 * h + 1) * HEAD_SIZE : (2 * h + 2) * HEAD_SIZE]


def placed_grads(mine, theirs):
    whole = pl.BlockSpec(memory_space=pltpu.VMEM)
    out = jax.ShapeDtypeStruct(mine.shape, jnp.bfloat16)
    return pl.pallas_call(
        place_kernel,
        name="place",
        in_specs=[whole, whole],
        out_specs=[whole, whole],
        out_shape=[out, out],
    )(*in_vmem(mine, theirs))


def local(queries, keys, values, grad_out):
    half, kv_width = keys.shape
    kv_heads = kv_width // HEAD_SIZE
    rows = 2 * half
    peers = lax.axis_size("ctx")
    pairs = peers // 2
    assert half == STRIDE and W == 2 * rows and peers % 2 == 0 and kv_heads % (2 * CHUNKS) == 0
    core, _ = pair_position()

    def swap(x):
        return lax.ppermute(x, "ctx", [(i, i ^ 1) for i in range(peers)])

    def shifted(x, by, wrap=True):
        pairs_sent = [(i, (i + by) % peers) for i in range(peers)]
        return lax.ppermute(x, "ctx", [(i, j) for i, j in pairs_sent if wrap or j == i + by])

    def exchanged(x):
        groups = [list(range(parity, peers, 2)) for parity in range(2)]
        return lax.all_to_all(x, "ctx", 0, 0, axis_index_groups=groups)

    def joined(mine, theirs):
        return jnp.where(
            core == 0,
            jnp.concatenate([mine, theirs], axis=1),
            jnp.concatenate([theirs, mine], axis=1),
        )

    sent = own_rows(keys, values, peers)
    k_other, v_other, sent = lax.optimization_barrier((swap(keys), swap(values), sent))
    far = lax.all_to_all(sent, "ctx", 0, 0, tiled=True)
    here = [arrange(keys, values, k_other, v_other, chunk) for chunk in range(CHUNKS)]
    near, past = [], []
    for chunk in range(CHUNKS):
        payload = here[chunk]
        if chunk > 0:
            payload, _ = lax.optimization_barrier((payload, far))
        near.append(shifted(payload, 2))
        past.append(shifted(payload, 4))
    q_sent, o_sent, _ = lax.optimization_barrier((queries, grad_out, here[0]))
    q_other, o_other = swap(q_sent), swap(o_sent)

    width = queries.shape[1] // (2 * CHUNKS)
    operands = (queries, q_other, grad_out, o_other, *here)
    dq_own, dq_other, norms, sums = [], [], [], []
    far_terms = None
    for chunk in range(CHUNKS):
        out = attention(chunk, operands, near[chunk], past[chunk], far, far_terms, width)
        if chunk == 0:
            staged = out[7:]
        operands = staged[3 * chunk : 3 * chunk + 3]
        last = chunk == CHUNKS - 1
        sums.append((out[3], shifted(out[4], -2, last), shifted(out[5], -4, last)))
        dq_own.append(out[0])
        dq_other.append(swap(out[1]))
        norms.append(out[2])
        far, _ = lax.optimization_barrier((far, out[2]))
        far_terms = out[6]

    terms, *_ = lax.optimization_barrier((far_terms, *sums[0][1:]))
    strided_terms = exchanged(terms.reshape(pairs, 2, kv_heads, HEAD_SIZE))
    grad_queries = joined(jnp.concatenate(dq_own, axis=1), jnp.concatenate(dq_other, axis=1))
    norm = jnp.concatenate(norms, axis=0)
    norm_sent, *_ = lax.optimization_barrier((norm[:, half:], *sums[0][1:]))
    log_norm = joined(norm[:, :half].T, swap(norm_sent).T)
    own, grad_queries, log_norm = lax.optimization_barrier((sums[-1][0], grad_queries, log_norm))
    terms = [x for chunk in sums[:-1] for x in chunk] + [own, *sums[-1][1:]]
    mine, theirs = collect(terms, strided_terms)
    grad_keys, grad_values = placed_grads(mine, swap(theirs))
    return (grad_queries, grad_keys, grad_values, log_norm)


def solution(mesh):
    placed = P(("groups", "ctx"), "head")
    return jax.shard_map(
        local,
        mesh=mesh,
        in_specs=(placed,) * 4,
        out_specs=(placed,) * 4,
        check_vma=False,
    )
```

```python
import functools
import math

import jax
import jax.numpy as jnp
from jax import lax
from jax.experimental import pallas as pl
from jax.experimental.pallas import tpu as pltpu
from jax.sharding import PartitionSpec as P

HEAD_SIZE = 128
W = 512
STRIDE = 128
CHUNKS = 2

NEG_FILL = -1e30
SCALE = 1.0 / math.sqrt(HEAD_SIZE)


def vmem_shape(shape, dtype):
    return pltpu.VMEM(shape, dtype)


def in_hbm(*arrays):
    return [pltpu.with_memory_space_constraint(x, pltpu.HBM) for x in arrays]


def in_vmem(*arrays):
    return [pltpu.with_memory_space_constraint(x, pltpu.VMEM) for x in arrays]


def head_columns(which, width=HEAD_SIZE):
    return pl.ds(pl.multiple_of(which * width, width), width)


def pair_position():
    index = lax.axis_index("ctx")
    return index & 1, index >> 1


def dot_nt(left, right):
    return lax.dot_general(
        left, right, (((1,), (1,)), ((), ())), preferred_element_type=jnp.float32
    )


def dot_nn(left, right):
    return lax.dot_general(
        left, right, (((1,), (0,)), ((), ())), preferred_element_type=jnp.float32
    )


def dot_tn(left, right):
    return lax.dot_general(
        left, right, (((0,), (0,)), ((), ())), preferred_element_type=jnp.float32
    )


def attend(
    chunk,
    staged_q,
    staged_o,
    here,
    kv_near,
    kv_past,
    kv_far,
    dq_own,
    dq_other,
    norm,
    g_here,
    g_near,
    g_past,
    g_far,
):
    half = staged_q.shape[1]
    rows = 2 * half
    far_rows = kv_far.shape[0]
    both = 2 * HEAD_SIZE
    count = kv_near.shape[1] // both
    width = dq_own.shape[1]
    heads = width // (count * HEAD_SIZE)
    core, pair = pair_position()
    wide = (half, rows)
    lane = lax.broadcasted_iota(jnp.int32, wide, 1) % half
    lower = lax.broadcasted_iota(jnp.int32, wide, 0) <= lane
    far_at = lax.broadcasted_iota(jnp.int32, (far_rows, rows), 0)
    far_lane = lax.broadcasted_iota(jnp.int32, (far_rows, rows), 1) % half
    far_token = far_at * half
    near_bias = jnp.where(pair >= 1, 0.0, NEG_FILL)
    past_bias = jnp.where(pair >= 2, 0.0, NEG_FILL)
    sides = []
    for side in range(2):
        later = core if side == 0 else 1 - core
        sides.append(
            (
                later,
                far_token <= pair * rows + later * half + far_lane - W,
                jnp.where(later == 0, past_bias, 0.0),
            )
        )

    def keys_of(at, side, which):
        columns = slice((2 * at + which) * HEAD_SIZE, (2 * at + which + 1) * HEAD_SIZE)
        far_row = 2 * (chunk * count + at) + which
        same = slice(side * half, (side + 1) * half)
        cross = slice((1 - side) * half, (2 - side) * half)
        full = jnp.where(sides[side][0] == 1, here[cross, columns], kv_past[cross, columns])
        return jnp.concatenate(
            [
                here[same, columns],
                kv_past[same, columns],
                full,
                kv_near[:, columns],
                kv_far[:, far_row, :],
            ],
            axis=0,
        )

    def operands(at, side, first):
        query, grad = (
            jnp.concatenate(
                [
                    staged[side, :, head * HEAD_SIZE : (head + 1) * HEAD_SIZE]
                    for head in (at * heads + first, at * heads + first + 1)
                ],
                axis=0,
            )
            for staged in (staged_q, staged_o)
        )
        key_all, value_all = keys_of(at, side, 0), keys_of(at, side, 1)
        return query, grad, key_all, dot_nt(key_all, query), dot_nt(value_all, grad)

    def merged(whole, bias):
        edge = jnp.where(lower, whole[:half], whole[half:rows] + bias)
        return edge, whole[rows : rows + half], whole[rows + half : 2 * rows + half]

    def reduced(op, parts):
        out = [op(part, axis=0, keepdims=True) for part in parts]
        return out

    def weights(at, side, first, score, dprob):
        _, far_open, full_bias = sides[side]
        edge, full, near = merged(score, past_bias)
        parts = [
            edge,
            full + full_bias,
            near + near_bias,
            jnp.where(far_open, score[2 * rows + half :], NEG_FILL),
        ]
        top = functools.reduce(jnp.maximum, reduced(jnp.max, parts))
        parts = [jnp.exp2((part - top) * (SCALE * math.log2(math.e))) for part in parts]
        total = sum(reduced(jnp.sum, parts))
        log_total = top * SCALE + jnp.log(total)
        for k in range(2):
            row = at * heads + first + k
            norm[row : row + 1, side * half : (side + 1) * half] = log_total[
                :, k * half : (k + 1) * half
            ]
        inverse = 1.0 / total
        parts = [part * inverse for part in parts]
        d_parts = [*merged(dprob, 0.0), dprob[2 * rows + half :]]
        delta = sum(reduced(jnp.sum, [part * d_part for part, d_part in zip(parts, d_parts)]))
        d_parts = [part * (d_part - delta) for part, d_part in zip(parts, d_parts)]

        def split(edge, *others):
            return jnp.concatenate(
                [
                    jnp.where(lower, edge, 0.0).astype(jnp.bfloat16),
                    jnp.where(lower, 0.0, edge).astype(jnp.bfloat16),
                    *(part.astype(jnp.bfloat16) for part in others),
                ],
                axis=0,
            )

        return split(*parts), split(*d_parts)

    steps = [
        (at, side, first)
        for at in range(count)
        for side in range(2)
        for first in range(0, heads, 2)
    ]
    following = operands(*steps[0])
    terms = {}
    for number, (at, side, first) in enumerate(steps):
        query, grad, key_all, score, dprob = following
        if number + 1 < len(steps):
            following = operands(*steps[number + 1])
        prob, dscore = weights(at, side, first, score, dprob)
        new = (dot_nn(dscore, query), dot_nn(prob, grad))
        terms[side] = new if first == 0 else tuple(a + b for a, b in zip(terms[side], new))
        query_term = (dot_tn(key_all, dscore) * SCALE).T.astype(jnp.bfloat16)
        dq_side = dq_own if side == 0 else dq_other
        for k in range(2):
            columns = slice(
                (at * heads + first + k) * HEAD_SIZE, (at * heads + first + k + 1) * HEAD_SIZE
            )
            dq_side[:, columns] = query_term[k * half : (k + 1) * half]
        if side == 1 and first + 2 == heads:
            for which in range(2):
                scale = SCALE if which == 0 else 1.0
                columns = slice((2 * at + which) * HEAD_SIZE, (2 * at + which + 1) * HEAD_SIZE)
                own, other = (terms[k][which] * scale for k in range(2))
                for k, (mine, theirs) in enumerate(((own, other), (other, own))):
                    cross = theirs[rows : rows + half]
                    here_too = sides[1 - k][0] == 1
                    place = slice(k * half, (k + 1) * half)
                    g_here[place, columns] = mine[:half] + jnp.where(here_too, cross, 0.0)
                    g_past[place, columns] = (
                        mine[half:rows] + jnp.where(here_too, 0.0, cross)
                    ).astype(jnp.bfloat16)
                joint = own[rows + half :] + other[rows + half :]
                g_near[:, columns] = joint[:rows].astype(jnp.bfloat16)
                g_far[:, 2 * (chunk * count + at) + which, :] = joint[rows:]


def stage_copies(chunk, sources, targets, done):
    q_own, q_other, o_own, o_other = sources[:4]
    staged_q, staged_o, here = targets
    core, _ = pair_position()
    columns = head_columns(core * CHUNKS + chunk, staged_q.shape[2])
    pieces = [
        (sources[4 + chunk], here),
        (q_own.at[:, columns], staged_q.at[0]),
        (o_own.at[:, columns], staged_o.at[0]),
        (q_other.at[:, columns], staged_q.at[1]),
        (o_other.at[:, columns], staged_o.at[1]),
    ]
    return [
        pltpu.make_async_copy(source, target, done.at[chunk, number])
        for number, (source, target) in enumerate(pieces)
    ]


def first_kernel(*refs):
    sources, blocks, outs = refs[: 4 + CHUNKS], refs[4 + CHUNKS : 7 + CHUNKS], refs[7 + CHUNKS :]
    mine, *later = (
        stage_copies(chunk, sources, targets, outs[-1])
        for chunk, targets in enumerate(
            [outs[-4:-1]] + [outs[7 + 3 * k : 10 + 3 * k] for k in range(CHUNKS - 1)]
        )
    )
    for copy in mine + sum(later, []):
        copy.start()
    for copy in mine:
        copy.wait()
    attend(0, *outs[-4:-1], *blocks, *outs[:7])
    for copy in sum(later, []):
        copy.wait()


def later_kernel(chunk, *refs):
    before, g_far = refs[6], refs[-1]
    g_far[:, : before.shape[1], :] = before[...]
    attend(chunk, *refs[:6], *refs[7:])


def attention(chunk, operands, kv_near, kv_past, kv_far, far_terms, width):
    half = kv_near.shape[0] // 2
    rows = 2 * half
    far_rows = kv_far.shape[0]
    both = 2 * HEAD_SIZE
    count = kv_near.shape[1] // both
    heads = width // (count * HEAD_SIZE)
    whole = pl.BlockSpec(memory_space=pltpu.VMEM)
    keys_seen = 3 * rows + far_rows
    staged = [(2, half, width), (2, half, width), (rows, count * both)]
    outs = [
        vmem_shape((half, width), jnp.bfloat16),
        vmem_shape((half, width), jnp.bfloat16),
        vmem_shape((count * heads, rows), jnp.float32),
        vmem_shape((rows, count * both), jnp.float32),
        vmem_shape((rows, count * both), jnp.bfloat16),
        vmem_shape((rows, count * both), jnp.bfloat16),
        vmem_shape((far_rows, 2 * count * (chunk + 1), HEAD_SIZE), jnp.float32),
    ]
    blocks = [kv_near, kv_past, kv_far]
    if chunk == 0:
        outs += [vmem_shape(shape, jnp.bfloat16) for shape in staged] * (CHUNKS - 1)
        operands = in_hbm(*operands)
        scratch = [pltpu.VMEM(shape, jnp.bfloat16) for shape in staged]
        scratch.append(pltpu.SemaphoreType.DMA((CHUNKS, 5)))
    else:
        operands = in_vmem(*operands)
        blocks.append(far_terms)
        scratch = []
    space = pl.BlockSpec(memory_space=pl.ANY) if chunk == 0 else whole
    return pl.pallas_call(
        first_kernel if chunk == 0 else functools.partial(later_kernel, chunk),
        name=f"attention_{chunk}",
        in_specs=[space] * len(operands) + [whole] * len(blocks),
        out_specs=[whole] * len(outs),
        out_shape=outs,
        scratch_shapes=scratch,
        compiler_params=pltpu.CompilerParams(vmem_limit_bytes=12 * 1024 * 1024),
        cost_estimate=pl.CostEstimate(
            flops=count * heads * rows * keys_seen * HEAD_SIZE * 20,
            transcendentals=count * heads * rows * keys_seen,
            bytes_accessed=6 * half * width * 2 + count * 5 * rows * both * 4,
        ),
    )(*operands, *in_vmem(*blocks))


def arrange_kernel(chunk, keys, values, k_other, v_other, payload):
    half = keys.shape[0]
    core, _ = pair_position()
    count = payload.shape[1] // (2 * HEAD_SIZE)
    for h in range(count):
        source = head_columns(core * (count * CHUNKS) + chunk * count + h)
        for side, (mine, theirs) in enumerate(((keys, k_other), (values, v_other))):
            to = slice((2 * h + side) * HEAD_SIZE, (2 * h + side + 1) * HEAD_SIZE)
            payload[:half, to] = mine[:, source]
            payload[half:, to] = theirs[:, source]


def arrange(keys, values, k_other, v_other, chunk):
    half, kv_width = keys.shape
    whole = pl.BlockSpec(memory_space=pltpu.VMEM)
    return pl.pallas_call(
        functools.partial(arrange_kernel, chunk),
        name=f"arrange_{chunk}",
        grid=(1,),
        in_specs=[pl.BlockSpec(keys.shape, lambda i: (0, 0))] * 2 + [whole] * 2,
        out_specs=whole,
        out_shape=pltpu.HBM((2 * half, kv_width // CHUNKS), keys.dtype),
    )(keys, values, *in_vmem(k_other, v_other))


def own_rows_kernel(keys, values, out):
    per_core = out.shape[1] // 2
    for core in range(2):
        rows = []
        for h in range(core * per_core, (core + 1) * per_core):
            columns = slice(h * HEAD_SIZE, (h + 1) * HEAD_SIZE)
            rows += [keys[0:1, columns], values[0:1, columns]]
        block = jnp.concatenate([row.astype(jnp.float32) for row in rows], axis=0)
        for peer in range(core, out.shape[0], 2):
            out[peer] = block.astype(out.dtype)


def own_rows(keys, values, peers):
    kv_width = keys.shape[1]
    head = pl.BlockSpec((16, kv_width), lambda i: (0, 0))
    shape = (peers, kv_width // HEAD_SIZE, HEAD_SIZE)
    return pl.pallas_call(
        own_rows_kernel,
        name="own_rows",
        grid=(1,),
        in_specs=[head, head],
        out_specs=pl.BlockSpec(shape, lambda i: (0, 0, 0)),
        out_shape=jax.ShapeDtypeStruct(shape, keys.dtype),
    )(keys, values)


def collect_kernel(*refs):
    *terms, strided, mine, theirs = refs
    half = mine.shape[0]
    width = terms[0].shape[1]
    core, _ = pair_position()
    own, other = (
        jnp.concatenate(
            [
                jnp.sum(strided[:, k, column, :], axis=0, keepdims=True)
                for column in range(strided.shape[2])
            ],
            axis=1,
        )
        for k in range(2)
    )
    extra = jnp.where(
        core == 0, jnp.concatenate([own, other], axis=0), jnp.concatenate([other, own], axis=0)
    )
    row = lax.broadcasted_iota(jnp.int32, (half, 1), 0)
    for chunk in range(CHUNKS):
        here, near, past = terms[3 * chunk : 3 * chunk + 3]
        columns = slice(chunk * width, (chunk + 1) * width)
        total = here[...] + near[...].astype(jnp.float32) + past[...].astype(jnp.float32)
        for k, out in enumerate((mine, theirs)):
            added = jnp.where(row == 0, extra[k : k + 1, columns], 0.0)
            out[:, columns] = (total[k * half : (k + 1) * half] + added).astype(out.dtype)


def collect(terms, strided):
    rows, width = terms[0].shape
    half = vmem_shape((rows // 2, CHUNKS * width), jnp.bfloat16)
    whole = pl.BlockSpec(memory_space=pltpu.VMEM)
    return pl.pallas_call(
        collect_kernel,
        name="collect",
        in_specs=[whole] * (len(terms) + 1),
        out_specs=[whole, whole],
        out_shape=[half, half],
        cost_estimate=pl.CostEstimate(
            flops=CHUNKS * rows * width * 4,
            transcendentals=0,
            bytes_accessed=CHUNKS * rows * width * 10,
        ),
    )(*in_vmem(*terms, strided))


def place_kernel(mine, theirs, grad_keys, grad_values):
    here, _ = pair_position()
    count = mine.shape[1] // (2 * HEAD_SIZE)
    for h in range(count):
        for core, block in ((here, mine), (1 - here, theirs)):
            to = head_columns(core * count + h)
            grad_keys[:, to] = block[:, 2 * h * HEAD_SIZE : (2 * h + 1) * HEAD_SIZE]
            grad_values[:, to] = block[:, (2 * h + 1) * HEAD_SIZE : (2 * h + 2) * HEAD_SIZE]


def placed_grads(mine, theirs):
    whole = pl.BlockSpec(memory_space=pltpu.VMEM)
    out = jax.ShapeDtypeStruct(mine.shape, jnp.bfloat16)
    return pl.pallas_call(
        place_kernel,
        name="place",
        in_specs=[whole, whole],
        out_specs=[whole, whole],
        out_shape=[out, out],
    )(*in_vmem(mine, theirs))


def local(queries, keys, values, grad_out):
    half, kv_width = keys.shape
    kv_heads = kv_width // HEAD_SIZE
    rows = 2 * half
    peers = lax.axis_size("ctx")
    pairs = peers // 2
    assert half == STRIDE and W == 2 * rows and peers % 2 == 0 and kv_heads % (2 * CHUNKS) == 0
    core, _ = pair_position()

    def swap(x):
        return lax.ppermute(x, "ctx", [(i, i ^ 1) for i in range(peers)])

    def shifted(x, by, wrap=True):
        pairs_sent = [(i, (i + by) % peers) for i in range(peers)]
        return lax.ppermute(x, "ctx", [(i, j) for i, j in pairs_sent if wrap or j == i + by])

    def exchanged(x):
        groups = [list(range(parity, peers, 2)) for parity in range(2)]
        return lax.all_to_all(x, "ctx", 0, 0, axis_index_groups=groups)

    def joined(mine, theirs):
        return jnp.where(
            core == 0,
            jnp.concatenate([mine, theirs], axis=1),
            jnp.concatenate([theirs, mine], axis=1),
        )

    sent = own_rows(keys, values, peers)
    k_other, v_other, sent = lax.optimization_barrier((swap(keys), swap(values), sent))
    far = lax.all_to_all(sent, "ctx", 0, 0, tiled=True)
    here = [arrange(keys, values, k_other, v_other, chunk) for chunk in range(CHUNKS)]
    near, past = [], []
    for chunk in range(CHUNKS):
        payload = here[chunk]
        if chunk > 0:
            payload, _ = lax.optimization_barrier((payload, far))
        near.append(shifted(payload, 2))
        past.append(shifted(payload, 4))
    q_sent, o_sent, _ = lax.optimization_barrier((queries, grad_out, here[0]))
    q_other, o_other = swap(q_sent), swap(o_sent)

    width = queries.shape[1] // (2 * CHUNKS)
    operands = (queries, q_other, grad_out, o_other, *here)
    dq_own, dq_other, norms, sums = [], [], [], []
    far_terms = None
    for chunk in range(CHUNKS):
        out = attention(chunk, operands, near[chunk], past[chunk], far, far_terms, width)
        if chunk == 0:
            staged = out[7:]
        operands = staged[3 * chunk : 3 * chunk + 3]
        last = chunk == CHUNKS - 1
        sums.append((out[3], shifted(out[4], -2, last), shifted(out[5], -4, last)))
        dq_own.append(out[0])
        dq_other.append(swap(out[1]))
        norms.append(out[2])
        far, _ = lax.optimization_barrier((far, out[2]))
        far_terms = out[6]

    terms, *_ = lax.optimization_barrier((far_terms, *sums[0][1:]))
    strided_terms = exchanged(terms.reshape(pairs, 2, kv_heads, HEAD_SIZE))
    grad_queries = joined(jnp.concatenate(dq_own, axis=1), jnp.concatenate(dq_other, axis=1))
    norm = jnp.concatenate(norms, axis=0)
    norm_sent, *_ = lax.optimization_barrier((norm[:, half:], *sums[0][1:]))
    log_norm = joined(norm[:, :half].T, swap(norm_sent).T)
    own, grad_queries, log_norm = lax.optimization_barrier((sums[-1][0], grad_queries, log_norm))
    terms = [x for chunk in sums[:-1] for x in chunk] + [own, *sums[-1][1:]]
    mine, theirs = collect(terms, strided_terms)
    grad_keys, grad_values = placed_grads(mine, swap(theirs))
    return (grad_queries, grad_keys, grad_values, log_norm)


def solution(mesh):
    placed = P(("groups", "ctx"), "head")
    return jax.shard_map(
        local,
        mesh=mesh,
        in_specs=(placed,) * 4,
        out_specs=(placed,) * 4,
        check_vma=False,
    )
```
